512 devices in a mesh: quad: 16 (over y, x), tile: 32 (over z, core).
Axes of the slice: x: 4, y: 4, z: 16, core: 2. Of those that a mesh axis runs over, the one named last changes fastest.
Arguments:
- blocks: bfloat16 [2048, 6, 256, 256], P(('quad', 'tile')), may hold values from -4 to 4
- offsets: int32 [2048, 6], P(('quad', 'tile')), may hold values from -3 to 3, as said below
- sketch: bfloat16 [524288, 512], P(('quad', 'tile')), may hold values from -6 to 6
- leaf_pivots: int32 [2048, 128], P(('quad', 'tile')), may hold values from 0 to 255, as said below
- node_pivots: int32 [512, 128], P(('quad', 'tile')), may hold values from 0 to 511, as said below
- pair_pivots: int32 [512, 64], P(('quad', 'tile')), may hold values from 0 to 127, as said below
- group_pivots: int32 [512, 32], P(('quad', 'tile')), may hold values from 0 to 63, as said below
Outputs:
- leaf_interp: float32 [524288, 128], P(('quad', 'tile'))
- node_interp: float32 [262144, 128], P(('quad', 'tile'))
- pair_interp: float32 [65536, 128], P(('quad', 'tile'))
- group_interp: float32 [32768, 128], P(('quad', 'tile'))
The draws below stay inside these ranges and needn't reach their ends.
Inputs may be any that keep to these rules, and one draw needn't show every extreme that they name: `offsets`: each row holds distinct values in rising order. `leaf_pivots`: each row holds distinct values in rising order. `node_pivots`: each row holds distinct values in rising order. `pair_pivots`: each row holds distinct values in rising order. `group_pivots`: each row holds distinct values in rising order.
All inputs are finite; a program needn't handle non-finite values.
Results may differ from the reference program's by a relative error of at most 0.0003.
Values may be sent and summed in bfloat16 or wider, within the bound.
A program may use at most 64 MiB of HBM per device.

```python
import math
import jax
import jax.numpy as jnp
from jax import lax

BLOCK = 256
SKETCH = 512
SKEL = 128
NNZ = 6
HALF = 3
LEAF_DEV = 4
NODES = 512
NPT = 2048


def choose_rows(key, count, total, keep):
    keys = jax.random.split(key, count)

    def one_row(single):
        return jnp.sort(jax.random.permutation(single, total)[:keep])
    return jax.vmap(one_row)(keys).astype(jnp.int32)


def draw_blocks(key, part):
    rough_key, row_key, col_key = jax.random.split(jax.random.fold_in(key, 21), 3)
    full_shape = (NPT, NNZ, BLOCK, BLOCK)
    spread = (BLOCK * NNZ) ** (-0.5)
    rough_part = jax.random.truncated_normal(rough_key, -6.0, 6.0, full_shape, jnp.float32) * spread
    strength = jnp.ones((NPT, 1, 1, 1), jnp.float32)
    row_phase = jax.random.uniform(row_key, (NPT, 24), jnp.float32, -math.pi, math.pi)
    col_phase = jax.random.uniform(col_key, (NPT, NNZ, 24), jnp.float32, -math.pi, math.pi)
    position = (jnp.arange(BLOCK, dtype=jnp.float32) + 0.5) * (math.pi / BLOCK)
    smooth = jnp.ones(full_shape, jnp.float32)
    for harmonic in range(1, 25):
        weight = 0.9 ** harmonic
        row_wave = jnp.cos(harmonic * position[None, :] + row_phase[:, harmonic - 1:harmonic])
        col_wave = jnp.cos(harmonic * position[None, None, :] + col_phase[:, :, harmonic - 1:harmonic])
        smooth = smooth + weight * row_wave[:, None, :, None] * col_wave[:, :, None, :]
    return (rough_part + 2.0 * spread * strength * smooth).astype(jnp.bfloat16)


def draw_offsets(key, part):
    return choose_rows(jax.random.fold_in(key, 11), NPT, 2 * HALF + 1, NNZ) - HALF


def draw_leaf_pivots(key, part):
    return choose_rows(jax.random.fold_in(key, 12), NPT, BLOCK, SKEL)


def draw_node_pivots(key, part):
    return choose_rows(jax.random.fold_in(key, 13), NODES, LEAF_DEV * SKEL, SKEL)


def draw_pair_pivots(key, part):
    return choose_rows(jax.random.fold_in(key, 14), NODES, SKEL, SKEL // 2)


def draw_group_pivots(key, part):
    return choose_rows(jax.random.fold_in(key, 15), NODES, SKEL // 2, SKEL // 4)


def block_scale(rng, shape, shards, smallest, largest):
    gain, own = 1.0, jax.random.fold_in(rng, 6)
    for axis_at, parts in shards:
        heights = jnp.exp(jax.random.uniform(jax.random.fold_in(own, axis_at), (parts,), jnp.float32, smallest / len(shards), largest / len(shards)))
        gain = gain * jnp.repeat(heights, shape[axis_at] // parts).reshape([-1 if axis == axis_at else 1 for axis in range(len(shape))])
    return gain


def gaussian(own_key, shape, scale, most, cuts=(), kind=jnp.bfloat16):
    gain = block_scale(own_key, shape, cuts, -0.22, 0.18) if cuts else 1.0
    drawn = jax.random.normal(own_key, shape, jnp.float32) * scale * gain
    return jnp.minimum(jnp.maximum(drawn, -most), most).astype(kind)


def setup_inputs(seed: int = 0) -> dict:
    splits = jax.random.split(jax.random.key(seed), 8)
    return {
        "blocks": draw_blocks(jax.random.fold_in(splits[7], 71), 0),
        "offsets": draw_offsets(jax.random.fold_in(splits[7], 71), 0),
        "sketch": gaussian(splits[2], (NPT * BLOCK, SKETCH), 1.0, 6.0, ((0, 512),)),
        "leaf_pivots": draw_leaf_pivots(jax.random.fold_in(splits[7], 71), 0),
        "node_pivots": draw_node_pivots(jax.random.fold_in(splits[7], 71), 0),
        "pair_pivots": draw_pair_pivots(jax.random.fold_in(splits[7], 71), 0),
        "group_pivots": draw_group_pivots(jax.random.fold_in(splits[7], 71), 0),
    }


def project(rows, skeleton):
    highest = lax.Precision.HIGHEST
    moment = jnp.dot(skeleton, skeleton.T, precision=highest)
    damping = jnp.sum(skeleton * skeleton) / skeleton.shape[0] + 1e-06
    matrix = moment + damping * jnp.eye(skeleton.shape[0], dtype=jnp.float32)
    coupling = jnp.dot(rows, skeleton.T, precision=highest)
    factor = jnp.linalg.cholesky(matrix)
    inner = lax.linalg.triangular_solve(factor, coupling.T, left_side=True, lower=True)
    outer = lax.linalg.triangular_solve(factor, inner, left_side=True, lower=True, transpose_a=True)
    return outer.T

def take_rows(rows, index):
    return jnp.take(rows, index, axis=0)

def reference(blocks, offsets, sketch, leaf_pivots, node_pivots, pair_pivots, group_pivots):
    margin = HALF * BLOCK
    padded = jnp.pad(sketch, ((margin, margin), (0, 0)))

    def one_node(items):
        node_blocks, node_offsets, node_leaf_pivots, node_pivot_row, node_index = items
        window = lax.dynamic_slice_in_dim(padded, (node_index * LEAF_DEV * BLOCK).astype(jnp.int32), (LEAF_DEV + 2 * HALF) * BLOCK, 0)
        panels = window.reshape(LEAF_DEV + 2 * HALF, BLOCK, SKETCH)
        source = jnp.arange(LEAF_DEV, dtype=jnp.int32)[:, None] + HALF + node_offsets
        gathered = panels[source].astype(jnp.float32)
        sample = jnp.einsum('pkab,pkbr->par', node_blocks.astype(jnp.float32), gathered)
        skeleton = jax.vmap(take_rows)(sample, node_leaf_pivots)
        leaf_part = jax.vmap(project)(sample, skeleton)
        stacked = skeleton.reshape(LEAF_DEV * SKEL, SKETCH)
        node_skel = take_rows(stacked, node_pivot_row)
        node_part = project(stacked, node_skel)
        return (leaf_part, node_part, node_skel)
    leaf_part, node_part, node_skel = lax.map(one_node, (blocks.reshape(NODES, LEAF_DEV, NNZ, BLOCK, BLOCK), offsets.reshape(NODES, LEAF_DEV, NNZ), leaf_pivots.reshape(NODES, LEAF_DEV, SKEL), node_pivots, jnp.arange(NODES, dtype=jnp.int32)))
    upper = jax.vmap(take_rows)(node_skel, pair_pivots)
    higher = jax.vmap(take_rows)(upper, group_pivots)
    pair_skel = jnp.repeat(upper.reshape(NODES // 2, SKEL, SKETCH), 2, axis=0)
    group_skel = jnp.repeat(higher.reshape(NODES // 4, SKEL, SKETCH), 4, axis=0)
    pair_part = jax.vmap(project)(node_skel, pair_skel)
    group_part = jax.vmap(project)(upper, group_skel)
    return (leaf_part.reshape(NPT * BLOCK, SKEL), node_part.reshape(NPT * SKEL, SKEL), pair_part.reshape(NODES * SKEL, SKEL), group_part.reshape(NODES * SKEL // 2, SKEL))
```

```python
import functools

import jax
import jax.numpy as jnp
from jax import lax
from jax.experimental import pallas as pl
from jax.experimental.pallas import tpu as pltpu
from jax.sharding import PartitionSpec as P

HALF = 3
NNZ = 6
LEAVES = 4
BLOCK = 256
SKEL = 128
COLS = 512
STEPS = 6

F32 = jnp.float32
BF16 = jnp.bfloat16
MESH = pl.DeviceIdType.MESH
NN = (((1,), (0,)), ((), ()))
NT = (((1,), (1,)), ((), ()))


def dot(a, b, dims=NN):
    return lax.dot_general(a, b, dims, preferred_element_type=F32)


def dot_highest(a, b):
    return lax.dot_general(
        a, b, NN, precision=lax.Precision.HIGHEST, preferred_element_type=F32
    )


def split(x):
    high = x.astype(BF16)
    low = (x - high.astype(F32)).astype(BF16)
    return high, low


def eye():
    row = lax.broadcasted_iota(jnp.int32, (SKEL, SKEL), 0)
    col = lax.broadcasted_iota(jnp.int32, (SKEL, SKEL), 1)
    return row == col


def gram(rows_high, rows_low, skel_high, skel_low):
    count = rows_high.shape[0]
    left = jnp.concatenate([rows_high, rows_low], axis=0)
    right = jnp.concatenate([skel_high, skel_low], axis=0)
    full = dot(left, right, NT)
    return (full[:count, :SKEL] + full[count:, :SKEL]) + (
        full[:count, SKEL:] + full[count:, SKEL:]
    )


def normalized(moment):
    diagonal = eye()
    trace = jnp.sum(jnp.where(diagonal, moment, 0.0), keepdims=True)
    damping = trace / SKEL + 1e-06
    scale = 1.0 / (65.0 * damping)
    return (moment + jnp.where(diagonal, damping, 0.0)) * scale, scale


def invert(start_ref, pair_ref, which):
    for j in which:
        high, low = split(start_ref[j])
        identity = jnp.where(eye(), 1.0, 0.0).astype(BF16)
        pair_ref[j, :, 0:128] = high
        pair_ref[j, :, 128:256] = low
        pair_ref[j, :, 256:384] = identity
        pair_ref[j, :, 384:512] = jnp.zeros_like(identity)

    def step(_, rho):
        gain = 2.0 / (2.0 - rho * rho)
        for j in which:
            held = pair_ref[j]
            out = dot(held[:, :256], jnp.concatenate([held, held], axis=0))
            t = held[:, 0:128].astype(F32) + held[:, 128:256].astype(F32)
            x = held[:, 256:384].astype(F32) + held[:, 384:512].astype(F32)
            t = gain * (2.0 * t - (out[:, 0:128] + out[:, 128:256]))
            x = gain * (2.0 * x - (out[:, 256:384] + out[:, 384:512]))
            high, low = split(t)
            pair_ref[j, :, 0:128] = high
            pair_ref[j, :, 128:256] = low
            high, low = split(x)
            pair_ref[j, :, 256:384] = high
            pair_ref[j, :, 384:512] = low
        return gain - 1.0

    lax.fori_loop(0, STEPS, step, jnp.float32(128.0 / 130.0))
    inverses = []
    for j in which:
        held = pair_ref[j]
        x = held[:, 256:384].astype(F32) + held[:, 384:512].astype(F32)
        left = dot_highest(start_ref[j], x)
        rest = jnp.where(eye(), 1.0, 0.0) - left
        inverses.append(x + dot_highest(x, rest))
    return inverses


def kernel(
    quads, tiles,
    offsets_ref, leaf_ref, node_ref, pair_ref, group_ref, blocks_hbm, sketch_hbm,
    leaf_hbm, node_hbm, pairs_hbm, groups_hbm,
    window, mats, pivots, pick_leaf, pick_up, rows, skel, coupling, node_coupling, small_coupling,
    start, work, pair_buf, group_buf, node_skel,
    leaf_out, node_out, pairs_out, groups_out,
    local_sem, send_sem, recv_sem, up_send, up_recv, out_sem,
):
    q = lax.axis_index("quad")
    t = lax.axis_index("tile")
    me = q * tiles + t
    last = quads * tiles - 1
    odd = t % 2
    even = 1 - odd

    def at(flat):
        return (flat // tiles, flat % tiles)

    own = pltpu.make_async_copy(sketch_hbm, window.at[pl.ds(HALF, LEAVES)], local_sem.at[LEAVES])
    own.start()
    loads = [
        pltpu.make_async_copy(blocks_hbm.at[i], mats.at[i], local_sem.at[i]) for i in range(LEAVES)
    ]
    for load in loads:
        load.start()

    sibling = (q, t + 1 - 2 * odd)
    pair_of = t // 2
    other_pair = pair_of + 1 - 2 * (pair_of % 2)
    cousins = [(q, 2 * other_pair), (q, 2 * other_pair + 1)]
    partners = [sibling] + cousins

    barrier = pltpu.get_barrier_semaphore()

    @pl.when(me > 0)
    def _():
        pl.semaphore_signal(barrier, inc=1, device_id=at(me - 1), device_id_type=MESH)

    @pl.when(me < last)
    def _():
        pl.semaphore_signal(barrier, inc=1, device_id=at(me + 1), device_id_type=MESH)

    for partner in partners:
        pl.semaphore_signal(barrier, inc=1, device_id=partner, device_id_type=MESH)
    ends = jnp.where(me > 0, 1, 0) + jnp.where(me < last, 1, 0)
    pl.semaphore_wait(barrier, 3 + ends)

    def to_right(j):
        return pltpu.make_async_remote_copy(
            src_ref=sketch_hbm.at[LEAVES - 1 - j], dst_ref=window.at[HALF - 1 - j],
            send_sem=send_sem.at[j], recv_sem=recv_sem.at[HALF - 1 - j],
            device_id=at(me + 1), device_id_type=MESH,
        )

    def to_left(j):
        return pltpu.make_async_remote_copy(
            src_ref=sketch_hbm.at[j], dst_ref=window.at[HALF + LEAVES + j],
            send_sem=send_sem.at[HALF + j], recv_sem=recv_sem.at[HALF + j],
            device_id=at(me - 1), device_id_type=MESH,
        )

    @pl.when(me < last)
    def _():
        for j in range(HALF):
            to_right(j).start()

    @pl.when(me > 0)
    def _():
        for j in range(HALF):
            to_left(j).start()

    @pl.when(me == 0)
    def _():
        window[0:HALF] = jnp.zeros((HALF, BLOCK, COLS), BF16)

    @pl.when(me == last)
    def _():
        window[HALF + LEAVES:] = jnp.zeros((HALF, BLOCK, COLS), BF16)

    pivots[...] = jnp.full((8, 128), -1.0, F32)
    pivots[0:4, :] = leaf_ref[...].astype(F32)
    pivots[4:5, :] = node_ref[...].astype(F32)
    pivots[5:6, 0:64] = pair_ref[...].astype(F32)
    pivots[6:7, 0:32] = group_ref[...].astype(F32)

    def one_hot(row, width):
        down = jnp.broadcast_to(pivots[row:row + 1, :], (128, 128)).T
        down = jnp.concatenate([down] * (width // 128), axis=1)
        lane = lax.broadcasted_iota(jnp.int32, (128, width), 1).astype(F32)
        return jnp.where(down == lane, 1.0, 0.0).astype(BF16)

    for i in range(LEAVES):
        pick_leaf[i] = one_hot(i, BLOCK)
    node_pick = one_hot(4, LEAVES * SKEL)
    upper_pick = dot(one_hot(5, SKEL)[0:64], node_pick).astype(BF16)
    higher_pick = dot(one_hot(6, 128)[0:32, 0:64], upper_pick).astype(BF16)
    pick_up[0:128] = node_pick
    pick_up[128:192] = upper_pick
    pick_up[192:224] = higher_pick

    own.wait()

    def arrived(slot, index):
        return pltpu.make_async_remote_copy(
            src_ref=window.at[slot], dst_ref=window.at[slot],
            send_sem=send_sem.at[0], recv_sem=recv_sem.at[index],
            device_id=sibling, device_id_type=MESH,
        )

    for j in range(HALF):
        arrived(j + (HALF + LEAVES) * even, j + HALF * even).wait_recv()

    for s in range(LEAVES):
        i = even * (LEAVES - 1 - s) + odd * s
        if s > 0:
            @pl.when((me > 0) & (me < last))
            def _():
                arrived(even * (HALF - s) + odd * (HALF + LEAVES - 1 + s),
                        even * (HALF - s) + odd * (HALF - 1 + s)).wait_recv()
        pltpu.make_async_copy(blocks_hbm.at[i], mats.at[i], local_sem.at[i]).wait()
        total = jnp.zeros((BLOCK, COLS), F32)
        for k in range(NNZ):
            near = offsets_ref[i, k] == k - HALF
            panel = jnp.where(near, window[i + k], window[i + k + 1])
            total = total + dot(mats[i, k], panel)
        high, low = split(total)
        pick = pick_leaf[i]
        skel_high = dot(pick, high).astype(BF16)
        skel_low = dot(pick, low).astype(BF16)
        skel[0, i] = skel_high
        skel[1, i] = skel_low
        matrix, scale = normalized(gram(skel_high, skel_low, skel_high, skel_low))
        start[i] = matrix
        coupling[i] = gram(high, low, skel_high, skel_low) * scale

    all_high = skel[0].reshape(LEAVES * SKEL, COLS)
    all_low = skel[1].reshape(LEAVES * SKEL, COLS)
    up_high = dot(pick_up[...], all_high).astype(BF16)
    up_low = dot(pick_up[...], all_low).astype(BF16)
    place = t % 4
    pair_buf[odd, 0] = up_high[128:192]
    pair_buf[odd, 1] = up_low[128:192]
    group_buf[place, 0] = up_high[192:224]
    group_buf[place, 1] = up_low[192:224]
    node_skel[0] = up_high[0:128]
    node_skel[1] = up_low[0:128]

    sends = [
        pltpu.make_async_remote_copy(
            src_ref=pair_buf.at[odd], dst_ref=pair_buf.at[odd],
            send_sem=up_send.at[0], recv_sem=up_recv.at[0],
            device_id=sibling, device_id_type=MESH,
        )
    ]
    for n, partner in enumerate(partners):
        sends.append(
            pltpu.make_async_remote_copy(
                src_ref=group_buf.at[place], dst_ref=group_buf.at[place],
                send_sem=up_send.at[1 + n], recv_sem=up_recv.at[1 + place],
                device_id=partner, device_id_type=MESH,
            )
        )
    for send in sends:
        send.start()

    node_high = node_skel[0]
    node_low = node_skel[1]
    matrix, scale = normalized(gram(node_high, node_low, node_high, node_low))
    start[LEAVES] = matrix
    node_coupling[...] = gram(all_high, all_low, node_high, node_low) * scale

    inverses = invert(start, work, range(LEAVES + 1))
    for i in range(LEAVES):
        leaf_out[i] = dot_highest(coupling[i], inverses[i])
    node_out[...] = dot_highest(node_coupling[...], inverses[LEAVES])
    puts = [
        pltpu.make_async_copy(leaf_out, leaf_hbm, out_sem.at[0]),
        pltpu.make_async_copy(node_out, node_hbm, out_sem.at[1]),
    ]
    for put in puts:
        put.start()

    pltpu.make_async_remote_copy(
        src_ref=pair_buf.at[even], dst_ref=pair_buf.at[even],
        send_sem=up_send.at[0], recv_sem=up_recv.at[0],
        device_id=sibling, device_id_type=MESH,
    ).wait_recv()
    for n in range(1, 4):
        spot = (place + n) % 4
        pltpu.make_async_remote_copy(
            src_ref=group_buf.at[spot], dst_ref=group_buf.at[spot],
            send_sem=up_send.at[0], recv_sem=up_recv.at[1 + spot],
            device_id=sibling, device_id_type=MESH,
        ).wait_recv()

    pair_high = jnp.concatenate([pair_buf[0, 0], pair_buf[1, 0]], axis=0)
    pair_low = jnp.concatenate([pair_buf[0, 1], pair_buf[1, 1]], axis=0)
    group_high = jnp.concatenate([group_buf[g, 0] for g in range(4)], axis=0)
    group_low = jnp.concatenate([group_buf[g, 1] for g in range(4)], axis=0)
    matrix, scale = normalized(gram(pair_high, pair_low, pair_high, pair_low))
    start[5] = matrix
    small_coupling[0:128] = gram(node_skel[0], node_skel[1], pair_high, pair_low) * scale
    matrix, scale = normalized(gram(group_high, group_low, group_high, group_low))
    start[6] = matrix
    small_coupling[128:192] = gram(pair_buf[odd, 0], pair_buf[odd, 1], group_high, group_low) * scale
    inverses = invert(start, work, (5, 6))
    pairs_out[...] = dot_highest(small_coupling[0:128], inverses[0])
    groups_out[...] = dot_highest(small_coupling[128:192], inverses[1])
    more = [
        pltpu.make_async_copy(pairs_out, pairs_hbm, out_sem.at[2]),
        pltpu.make_async_copy(groups_out, groups_hbm, out_sem.at[3]),
    ]
    for put in more:
        put.start()

    @pl.when(me < last)
    def _():
        for j in range(HALF):
            to_right(j).wait_send()

    @pl.when(me > 0)
    def _():
        for j in range(HALF):
            to_left(j).wait_send()

    for send in sends:
        send.wait_send()
    for put in puts + more:
        put.wait()


def body(quads, tiles, blocks, offsets, sketch, leaf_pivots, node_pivots, pair_pivots, group_pivots):
    any_space = pl.BlockSpec(memory_space=pl.ANY)
    vmem = pl.BlockSpec(memory_space=pltpu.VMEM)
    shapes = [
        ((LEAVES, BLOCK, SKEL), F32),
        ((LEAVES * SKEL, SKEL), F32),
        ((SKEL, SKEL), F32),
        ((SKEL // 2, SKEL), F32),
    ]
    outs = pl.pallas_call(
        functools.partial(kernel, quads, tiles),
        out_shape=[jax.ShapeDtypeStruct(s, d) for s, d in shapes],
        in_specs=[pl.BlockSpec(memory_space=pltpu.SMEM), vmem, vmem, vmem, vmem, any_space, any_space],
        out_specs=[any_space] * 4,
        scratch_shapes=[
            pltpu.VMEM((LEAVES + 2 * HALF, BLOCK, COLS), BF16),
            pltpu.VMEM((LEAVES, NNZ, BLOCK, BLOCK), BF16),
            pltpu.VMEM((8, 128), F32),
            pltpu.VMEM((LEAVES, SKEL, BLOCK), BF16),
            pltpu.VMEM((224, LEAVES * SKEL), BF16),
            pltpu.VMEM((8, 128), F32),
            pltpu.VMEM((2, LEAVES, SKEL, COLS), BF16),
            pltpu.VMEM((LEAVES, BLOCK, SKEL), F32),
            pltpu.VMEM((LEAVES * SKEL, SKEL), F32),
            pltpu.VMEM((192, SKEL), F32),
            pltpu.VMEM((7, SKEL, SKEL), F32),
            pltpu.VMEM((7, SKEL, 4 * SKEL), BF16),
            pltpu.VMEM((2, 2, 64, COLS), BF16),
            pltpu.VMEM((4, 2, 32, COLS), BF16),
            pltpu.VMEM((2, SKEL, COLS), BF16),
            pltpu.VMEM((LEAVES, BLOCK, SKEL), F32),
            pltpu.VMEM((LEAVES * SKEL, SKEL), F32),
            pltpu.VMEM((SKEL, SKEL), F32),
            pltpu.VMEM((SKEL // 2, SKEL), F32),
            pltpu.SemaphoreType.DMA((LEAVES + 1,)),
            pltpu.SemaphoreType.DMA((2 * HALF,)),
            pltpu.SemaphoreType.DMA((2 * HALF,)),
            pltpu.SemaphoreType.DMA((4,)),
            pltpu.SemaphoreType.DMA((5,)),
            pltpu.SemaphoreType.DMA((4,)),
        ],
        compiler_params=pltpu.CompilerParams(collective_id=0, has_side_effects=True),
        name="compress",
    )(offsets, leaf_pivots, node_pivots, pair_pivots, group_pivots,
      blocks, sketch.reshape(LEAVES, BLOCK, COLS))
    return outs[0].reshape(LEAVES * BLOCK, SKEL), outs[1], outs[2], outs[3]


def solution(mesh):
    split_all = P(("quad", "tile"), None)
    placed = (P(("quad", "tile"), None, None, None),) + (split_all,) * 6
    run = functools.partial(body, mesh.shape["quad"], mesh.shape["tile"])
    return jax.shard_map(
        run, mesh=mesh, in_specs=placed, out_specs=(split_all,) * 4, check_vma=False
    )
```

```python
import functools

import jax
import jax.numpy as jnp
from jax import lax
from jax.experimental import pallas as pl
from jax.experimental.pallas import tpu as pltpu
from jax.sharding import PartitionSpec as P

HALF = 3
NNZ = 6
LEAVES = 4
BLOCK = 256
SKEL = 128
COLS = 512
STEPS = 6

F32 = jnp.float32
BF16 = jnp.bfloat16
MESH = pl.DeviceIdType.MESH
NN = (((1,), (0,)), ((), ()))
NT = (((1,), (1,)), ((), ()))


def dot(a, b, dims=NN):
    return lax.dot_general(a, b, dims, preferred_element_type=F32)


def dot_highest(a, b):
    return lax.dot_general(
        a, b, NN, precision=lax.Precision.HIGHEST, preferred_element_type=F32
    )


def split(x):
    high = x.astype(BF16)
    low = (x - high.astype(F32)).astype(BF16)
    return high, low


def eye():
    row = lax.broadcasted_iota(jnp.int32, (SKEL, SKEL), 0)
    col = lax.broadcasted_iota(jnp.int32, (SKEL, SKEL), 1)
    return row == col


def gram(rows_high, rows_low, skel_high, skel_low):
    count = rows_high.shape[0]
    left = jnp.concatenate([rows_high, rows_low], axis=0)
    right = jnp.concatenate([skel_high, skel_low], axis=0)
    full = dot(left, right, NT)
    return (full[:count, :SKEL] + full[count:, :SKEL]) + (
        full[:count, SKEL:] + full[count:, SKEL:]
    )


def normalized(moment):
    diagonal = eye()
    trace = jnp.sum(jnp.where(diagonal, moment, 0.0), keepdims=True)
    damping = trace / SKEL + 1e-06
    scale = 1.0 / (65.0 * damping)
    return (moment + jnp.where(diagonal, damping, 0.0)) * scale, scale


def invert(start_ref, pair_ref, which):
    for j in which:
        high, low = split(start_ref[j])
        identity = jnp.where(eye(), 1.0, 0.0).astype(BF16)
        pair_ref[j, :, 0:128] = high
        pair_ref[j, :, 128:256] = low
        pair_ref[j, :, 256:384] = identity
        pair_ref[j, :, 384:512] = jnp.zeros_like(identity)

    def step(_, rho):
        gain = 2.0 / (2.0 - rho * rho)
        for j in which:
            held = pair_ref[j]
            out = dot(held[:, :256], jnp.concatenate([held, held], axis=0))
            t = held[:, 0:128].astype(F32) + held[:, 128:256].astype(F32)
            x = held[:, 256:384].astype(F32) + held[:, 384:512].astype(F32)
            t = gain * (2.0 * t - (out[:, 0:128] + out[:, 128:256]))
            x = gain * (2.0 * x - (out[:, 256:384] + out[:, 384:512]))
            high, low = split(t)
            pair_ref[j, :, 0:128] = high
            pair_ref[j, :, 128:256] = low
            high, low = split(x)
            pair_ref[j, :, 256:384] = high
            pair_ref[j, :, 384:512] = low
        return gain - 1.0

    lax.fori_loop(0, STEPS, step, jnp.float32(128.0 / 130.0))
    inverses = []
    for j in which:
        held = pair_ref[j]
        x = held[:, 256:384].astype(F32) + held[:, 384:512].astype(F32)
        left = dot_highest(start_ref[j], x)
        rest = jnp.where(eye(), 1.0, 0.0) - left
        inverses.append(x + dot_highest(x, rest))
    return inverses


def kernel(
    quads, tiles,
    offsets_hbm, leaf_hbm, node_hbm, pair_hbm, group_hbm, blocks_hbm, sketch_hbm,
    leaf_result, node_result, node_rows, pair_rows, group_rows,
    window, mats, offsets, leaf_index, node_index, pair_index, group_index, pivots, pick_leaf, pick_up, pick_send, partial,
    skel, coupling, node_coupling, start, work, upper, higher, node_skel,
    leaf_out, node_out,
    local_sem, index_sem, send_sem, recv_sem, up_send, up_recv, out_sem,
):
    q = lax.axis_index("quad")
    t = lax.axis_index("tile")
    me = q * tiles + t
    last = quads * tiles - 1
    odd = t % 2
    even = 1 - odd

    def at(flat):
        return (flat // tiles, flat % tiles)

    sibling = (q, t + 1 - 2 * odd)
    pair_of = t // 2
    other_pair = pair_of + 1 - 2 * (pair_of % 2)
    cousins = [(q, 2 * other_pair), (q, 2 * other_pair + 1)]
    partners = cousins + [sibling]

    barrier = pltpu.get_barrier_semaphore()

    @pl.when(me > 0)
    def _():
        pl.semaphore_signal(barrier, inc=1, device_id=at(me - 1), device_id_type=MESH)

    @pl.when(me < last)
    def _():
        pl.semaphore_signal(barrier, inc=1, device_id=at(me + 1), device_id_type=MESH)

    for partner in partners:
        pl.semaphore_signal(barrier, inc=1, device_id=partner, device_id_type=MESH)

    smalls = [
        pltpu.make_async_copy(offsets_hbm, offsets, index_sem.at[0]),
        pltpu.make_async_copy(leaf_hbm, leaf_index, index_sem.at[1]),
        pltpu.make_async_copy(node_hbm, node_index, index_sem.at[2]),
        pltpu.make_async_copy(pair_hbm, pair_index, index_sem.at[3]),
        pltpu.make_async_copy(group_hbm, group_index, index_sem.at[4]),
    ]
    for small in smalls:
        small.start()
    own = pltpu.make_async_copy(sketch_hbm, window.at[pl.ds(HALF, LEAVES)], local_sem.at[LEAVES])
    own.start()

    def leaf_at(s):
        return even * (LEAVES - 1 - s) + odd * s

    def load(i):
        return pltpu.make_async_copy(blocks_hbm.at[i], mats.at[i], local_sem.at[i])

    for s in range(LEAVES):
        load(leaf_at(s)).start()

    ends = jnp.where(me > 0, 1, 0) + jnp.where(me < last, 1, 0)
    pl.semaphore_wait(barrier, 3 + ends)

    def to_right(j):
        return pltpu.make_async_remote_copy(
            src_ref=sketch_hbm.at[LEAVES - 1 - j], dst_ref=window.at[HALF - 1 - j],
            send_sem=send_sem.at[j], recv_sem=recv_sem.at[HALF - 1 - j],
            device_id=at(me + 1), device_id_type=MESH,
        )

    def to_left(j):
        return pltpu.make_async_remote_copy(
            src_ref=sketch_hbm.at[j], dst_ref=window.at[HALF + LEAVES + j],
            send_sem=send_sem.at[HALF + j], recv_sem=recv_sem.at[HALF + j],
            device_id=at(me - 1), device_id_type=MESH,
        )

    @pl.when(me < last)
    def _():
        for j in range(HALF):
            to_right(j).start()

    @pl.when(me > 0)
    def _():
        for j in range(HALF):
            to_left(j).start()

    @pl.when(me == 0)
    def _():
        window[0:HALF] = jnp.zeros((HALF, BLOCK, COLS), BF16)

    @pl.when(me == last)
    def _():
        window[HALF + LEAVES:] = jnp.zeros((HALF, BLOCK, COLS), BF16)

    for small in smalls:
        small.wait()
    pivots[...] = jnp.full((8, 128), -1.0, F32)
    pivots[0:4, :] = leaf_index[...].astype(F32)
    pivots[4:5, :] = node_index[...].astype(F32)
    pivots[5:6, 0:64] = pair_index[...].astype(F32)
    pivots[6:7, 0:32] = group_index[...].astype(F32)

    def one_hot(row, width):
        down = jnp.broadcast_to(pivots[row:row + 1, :], (128, 128)).T
        down = jnp.concatenate([down] * (width // 128), axis=1)
        lane = lax.broadcasted_iota(jnp.int32, (128, width), 1).astype(F32)
        return jnp.where(down == lane, 1.0, 0.0).astype(BF16)

    for i in range(LEAVES):
        pick_leaf[i] = one_hot(i, BLOCK)
    node_pick = one_hot(4, LEAVES * SKEL)
    upper_pick = dot(one_hot(5, SKEL)[0:64], node_pick).astype(BF16)
    higher_pick = dot(one_hot(6, 128)[0:32, 0:64], upper_pick).astype(BF16)
    pick_up[...] = node_pick
    both_pick = jnp.concatenate([upper_pick, higher_pick], axis=0)
    for i in range(LEAVES):
        pick_send[i] = dot(both_pick[:, i * SKEL:(i + 1) * SKEL], pick_leaf[i]).astype(BF16)
    partial[...] = jnp.zeros_like(partial)

    own.wait()

    def arrived(slot, which):
        return pltpu.make_async_remote_copy(
            src_ref=window.at[slot], dst_ref=window.at[slot],
            send_sem=send_sem.at[0], recv_sem=recv_sem.at[which],
            device_id=sibling, device_id_type=MESH,
        )

    for j in range(HALF):
        arrived(j + (HALF + LEAVES) * even, j + HALF * even).wait_recv()

    def term(i, j):
        k = even * (NNZ - 1 - j) + odd * j
        near = offsets[i, k] == k - HALF
        panel = jnp.where(near, window[i + k], window[i + k + 1])
        return dot(mats[i, k], panel)

    def first_terms(i):
        load(i).wait()
        total = term(i, 0)
        for j in range(1, NNZ - 1):
            total = total + term(i, j)
        return total

    def last_term(s, i, total):
        if s > 0:
            @pl.when((me > 0) & (me < last))
            def _():
                arrived(even * (HALF - s) + odd * (HALF + LEAVES - 1 + s),
                        even * (HALF - s) + odd * (HALF - 1 + s)).wait_recv()
        high, low = split(total + term(i, NNZ - 1))
        partial[0] += dot(pick_send[i], high)
        partial[1] += dot(pick_send[i], low)
        return high, low

    def leaf_stage(s, i, high, low):
        pick = pick_leaf[i]
        skel_high = dot(pick, high).astype(BF16)
        skel_low = dot(pick, low).astype(BF16)
        skel[0, i] = skel_high
        skel[1, i] = skel_low
        matrix, scale = normalized(gram(skel_high, skel_low, skel_high, skel_low))
        start[s] = matrix
        coupling[s] = gram(high, low, skel_high, skel_low) * scale

    def leaf_put(i):
        return pltpu.make_async_copy(leaf_out.at[i], leaf_result.at[i], out_sem.at[i])

    for s in range(LEAVES - 1):
        i = leaf_at(s)
        high, low = last_term(s, i, first_terms(i))
        leaf_stage(s, i, high, low)

    inverses = invert(start, work, range(LEAVES - 1))
    for s in range(LEAVES - 1):
        i = leaf_at(s)
        leaf_out[i] = dot_highest(coupling[s], inverses[s])
        leaf_put(i).start()

    s = LEAVES - 1
    i = leaf_at(s)
    high, low = last_term(s, i, first_terms(i))
    place = t % 4
    upper[0] = partial[0, 0:64].astype(BF16)
    upper[1] = partial[1, 0:64].astype(BF16)
    higher[0] = partial[0, 64:96].astype(BF16)
    higher[1] = partial[1, 64:96].astype(BF16)

    sends = []
    for n, partner in enumerate(partners):
        sends.append(
            pltpu.make_async_remote_copy(
                src_ref=higher, dst_ref=group_rows.at[place],
                send_sem=up_send.at[1 + n], recv_sem=up_recv.at[1 + place],
                device_id=partner, device_id_type=MESH,
            )
        )
    sends.append(
        pltpu.make_async_remote_copy(
            src_ref=upper, dst_ref=pair_rows.at[odd],
            send_sem=up_send.at[0], recv_sem=up_recv.at[0],
            device_id=sibling, device_id_type=MESH,
        )
    )
    for send in sends:
        send.start()
    keeps = [
        pltpu.make_async_copy(upper, pair_rows.at[odd], out_sem.at[5]),
        pltpu.make_async_copy(higher, group_rows.at[place], out_sem.at[6]),
    ]
    for keep in keeps:
        keep.start()

    leaf_stage(s, i, high, low)
    all_high = skel[0].reshape(LEAVES * SKEL, COLS)
    all_low = skel[1].reshape(LEAVES * SKEL, COLS)
    node_high = dot(pick_up[...], all_high).astype(BF16)
    node_low = dot(pick_up[...], all_low).astype(BF16)
    node_skel[0] = node_high
    node_skel[1] = node_low
    keeps.append(pltpu.make_async_copy(node_skel, node_rows, out_sem.at[7]))
    keeps[-1].start()
    matrix, scale = normalized(gram(node_high, node_low, node_high, node_low))
    start[LEAVES] = matrix
    node_coupling[...] = gram(all_high, all_low, node_high, node_low) * scale
    inverses = invert(start, work, (LEAVES - 1, LEAVES))
    leaf_out[i] = dot_highest(coupling[s], inverses[0])
    leaf_put(i).start()
    node_out[...] = dot_highest(node_coupling[...], inverses[1])
    keeps.append(pltpu.make_async_copy(node_out, node_result, out_sem.at[4]))
    keeps[-1].start()

    pltpu.make_async_remote_copy(
        src_ref=upper, dst_ref=pair_rows.at[even],
        send_sem=up_send.at[0], recv_sem=up_recv.at[0],
        device_id=sibling, device_id_type=MESH,
    ).wait_recv()
    for n in range(1, 4):
        spot = (place + n) % 4
        pltpu.make_async_remote_copy(
            src_ref=higher, dst_ref=group_rows.at[spot],
            send_sem=up_send.at[0], recv_sem=up_recv.at[1 + spot],
            device_id=sibling, device_id_type=MESH,
        ).wait_recv()

    @pl.when(me < last)
    def _():
        for j in range(HALF):
            to_right(j).wait_send()

    @pl.when(me > 0)
    def _():
        for j in range(HALF):
            to_left(j).wait_send()

    for send in sends:
        send.wait_send()
    for keep in keeps:
        keep.wait()
    for i in range(LEAVES):
        leaf_put(i).wait()


def finish(
    node_rows, pair_rows, group_rows, leaf_result, node_result,
    leaf_hbm, node_hbm, pairs_hbm, groups_hbm,
    node_skel, pair_buf, group_buf, leaf_out, node_out, small_coupling, start, work,
    pairs_out, groups_out, in_sem, out_sem,
):
    gets = [
        pltpu.make_async_copy(group_rows, group_buf, in_sem.at[0]),
        pltpu.make_async_copy(pair_rows, pair_buf, in_sem.at[1]),
        pltpu.make_async_copy(node_rows, node_skel, in_sem.at[2]),
        pltpu.make_async_copy(leaf_result, leaf_out, in_sem.at[3]),
        pltpu.make_async_copy(node_result, node_out, in_sem.at[4]),
    ]
    for get in gets:
        get.start()
    odd = lax.axis_index("tile") % 2
    gets[0].wait()
    group_high = jnp.concatenate([group_buf[g, 0] for g in range(4)], axis=0)
    group_low = jnp.concatenate([group_buf[g, 1] for g in range(4)], axis=0)
    matrix, scale = normalized(gram(group_high, group_low, group_high, group_low))
    start[1] = matrix
    gets[1].wait()
    pair_high = jnp.concatenate([pair_buf[0, 0], pair_buf[1, 0]], axis=0)
    pair_low = jnp.concatenate([pair_buf[0, 1], pair_buf[1, 1]], axis=0)
    small_coupling[128:192] = gram(pair_buf[odd, 0], pair_buf[odd, 1], group_high, group_low) * scale
    matrix, scale = normalized(gram(pair_high, pair_low, pair_high, pair_low))
    start[0] = matrix
    gets[2].wait()
    small_coupling[0:128] = gram(node_skel[0], node_skel[1], pair_high, pair_low) * scale
    gets[3].wait()
    gets[4].wait()
    puts = [
        pltpu.make_async_copy(leaf_out, leaf_hbm, out_sem.at[0]),
        pltpu.make_async_copy(node_out, node_hbm, out_sem.at[1]),
        pltpu.make_async_copy(pairs_out, pairs_hbm, out_sem.at[2]),
        pltpu.make_async_copy(groups_out, groups_hbm, out_sem.at[3]),
    ]
    puts[0].start()
    puts[1].start()
    inverses = invert(start, work, (0, 1))
    pairs_out[...] = dot_highest(small_coupling[0:128], inverses[0])
    puts[2].start()
    groups_out[...] = dot_highest(small_coupling[128:192], inverses[1])
    puts[3].start()
    for put in puts:
        put.wait()


def body(quads, tiles, blocks, offsets, sketch, leaf_pivots, node_pivots, pair_pivots, group_pivots):
    any_space = pl.BlockSpec(memory_space=pl.ANY)
    dma = pltpu.SemaphoreType.DMA
    leaf_shape = ((LEAVES, BLOCK, SKEL), F32)
    node_shape = ((LEAVES * SKEL, SKEL), F32)
    rows_shape = ((2, SKEL, COLS), BF16)
    pair_shape = ((2, 2, SKEL // 2, COLS), BF16)
    group_shape = ((4, 2, SKEL // 4, COLS), BF16)
    shapes = [leaf_shape, node_shape, rows_shape, pair_shape, group_shape]
    leaf_result, node_result, node_rows, pair_rows, group_rows = pl.pallas_call(
        functools.partial(kernel, quads, tiles),
        out_shape=[jax.ShapeDtypeStruct(s, d) for s, d in shapes],
        in_specs=[any_space] * 7,
        out_specs=[any_space] * 5,
        scratch_shapes=[
            pltpu.VMEM((LEAVES + 2 * HALF, BLOCK, COLS), BF16),
            pltpu.VMEM((LEAVES, NNZ, BLOCK, BLOCK), BF16),
            pltpu.SMEM((LEAVES, NNZ), jnp.int32),
            pltpu.VMEM((LEAVES, 128), jnp.int32),
            pltpu.VMEM((1, 128), jnp.int32),
            pltpu.VMEM((1, 64), jnp.int32),
            pltpu.VMEM((1, 32), jnp.int32),
            pltpu.VMEM((8, 128), F32),
            pltpu.VMEM((LEAVES, SKEL, BLOCK), BF16),
            pltpu.VMEM((SKEL, LEAVES * SKEL), BF16),
            pltpu.VMEM((LEAVES, 96, BLOCK), BF16),
            pltpu.VMEM((2, 96, COLS), F32),
            pltpu.VMEM((2, LEAVES, SKEL, COLS), BF16),
            pltpu.VMEM((LEAVES, BLOCK, SKEL), F32),
            pltpu.VMEM((LEAVES * SKEL, SKEL), F32),
            pltpu.VMEM((LEAVES + 1, SKEL, SKEL), F32),
            pltpu.VMEM((LEAVES + 1, SKEL, 4 * SKEL), BF16),
            pltpu.VMEM((2, SKEL // 2, COLS), BF16),
            pltpu.VMEM((2, SKEL // 4, COLS), BF16),
            pltpu.VMEM(*rows_shape),
            pltpu.VMEM(*leaf_shape),
            pltpu.VMEM(*node_shape),
            dma((LEAVES + 1,)), dma((5,)), dma((2 * HALF,)), dma((2 * HALF,)),
            dma((4,)), dma((5,)), dma((8,)),
        ],
        compiler_params=pltpu.CompilerParams(collective_id=0, has_side_effects=True),
        name="compress",
    )(offsets, leaf_pivots, node_pivots, pair_pivots, group_pivots,
      blocks, sketch.reshape(LEAVES, BLOCK, COLS))
    outs = [leaf_shape, node_shape, ((SKEL, SKEL), F32), ((SKEL // 2, SKEL), F32)]
    leaf, node, pairs, groups = pl.pallas_call(
        finish,
        out_shape=[jax.ShapeDtypeStruct(s, d) for s, d in outs],
        in_specs=[any_space] * 5,
        out_specs=[any_space] * 4,
        scratch_shapes=[
            pltpu.VMEM(*rows_shape),
            pltpu.VMEM(*pair_shape),
            pltpu.VMEM(*group_shape),
            pltpu.VMEM(*leaf_shape),
            pltpu.VMEM(*node_shape),
            pltpu.VMEM((192, SKEL), F32),
            pltpu.VMEM((2, SKEL, SKEL), F32),
            pltpu.VMEM((2, SKEL, 4 * SKEL), BF16),
            pltpu.VMEM((SKEL, SKEL), F32),
            pltpu.VMEM((SKEL // 2, SKEL), F32),
            dma((5,)), dma((4,)),
        ],
        name="finish",
    )(node_rows, pair_rows, group_rows, leaf_result, node_result)
    return leaf.reshape(LEAVES * BLOCK, SKEL), node, pairs, groups


def solution(mesh):
    split_all = P(("quad", "tile"), None)
    placed = (P(("quad", "tile"), None, None, None),) + (split_all,) * 6
    run = functools.partial(body, mesh.shape["quad"], mesh.shape["tile"])
    return jax.shard_map(
        run, mesh=mesh, in_specs=placed, out_specs=(split_all,) * 4, check_vma=False
    )
```

```python
import functools

import jax
import jax.numpy as jnp
from jax import lax
from jax.experimental import pallas as pl
from jax.experimental.pallas import tpu as pltpu
from jax.sharding import PartitionSpec as P

HALF = 3
NNZ = 6
LEAVES = 4
BLOCK = 256
SKEL = 128
COLS = 512
STEPS = 6

F32 = jnp.float32
BF16 = jnp.bfloat16
MESH = pl.DeviceIdType.MESH
NN = (((1,), (0,)), ((), ()))
NT = (((1,), (1,)), ((), ()))


def dot(a, b, dims=NN):
    return lax.dot_general(a, b, dims, preferred_element_type=F32)


def split(x):
    high = x.astype(BF16)
    low = (x - high.astype(F32)).astype(BF16)
    return high, low


def eye():
    row = lax.broadcasted_iota(jnp.int32, (SKEL, SKEL), 0)
    col = lax.broadcasted_iota(jnp.int32, (SKEL, SKEL), 1)
    return row == col


def gram(rows_high, rows_low, skel_high, skel_low):
    count = rows_high.shape[0]
    left = jnp.concatenate([rows_high, rows_low], axis=0)
    right = jnp.concatenate([skel_high, skel_low], axis=0)
    full = dot(left, right, NT)
    return (full[:count, :SKEL] + full[count:, :SKEL]) + (
        full[:count, SKEL:] + full[count:, SKEL:]
    )


def normalized(moment):
    diagonal = eye()
    trace = jnp.sum(jnp.where(diagonal, moment, 0.0), keepdims=True)
    damping = trace / SKEL + 1e-06
    scale = 1.0 / (65.0 * damping)
    return (moment + jnp.where(diagonal, damping, 0.0)) * scale, scale


def split3(x):
    high = x.astype(BF16)
    rest = x - high.astype(F32)
    middle = rest.astype(BF16)
    low = (rest - middle.astype(F32)).astype(BF16)
    return high, middle, low


def across(parts):
    return jnp.concatenate(parts, axis=1)


def down(parts):
    return jnp.concatenate(parts, axis=0)


def invert(matrices):
    unit = jnp.where(eye(), 1.0, 0.0)
    rho = 128.0 / 130.0
    ts = list(matrices)
    xs = [None] * len(ts)
    for step in range(STEPS):
        gain = 2.0 / (2.0 - rho * rho)
        rho = gain - 1.0
        for j, t in enumerate(ts):
            th, tl = split(t)
            left = across([th, tl, th])
            if step == 0:
                square = dot(left, down([th, th, tl]))
                xs[j] = gain * (2.0 * unit - t)
                ts[j] = gain * (2.0 * t - square)
                continue
            xh, xl = split(xs[j])
            if step == STEPS - 1:
                product = dot(left, down([xh, xh, xl]))
            else:
                both = dot(left, down([across([th, xh]), across([th, xh]), across([tl, xl])]))
                ts[j] = gain * (2.0 * t - both[:, :SKEL])
                product = both[:, SKEL:]
            xs[j] = gain * (2.0 * xs[j] - product)
    inverses = []
    for x, matrix in zip(xs, matrices):
        xh, xl = split(x)
        high, middle, low = split3(matrix)
        near = dot(across([high, middle, high, middle, low]), down([xh, xh, xl, xl, xh]))
        eh, el = split(unit - near)
        fix = dot(across([xh, xl, xh]), down([eh, eh, el]))
        inverses.append((xh.astype(F32) + xl.astype(F32)) + fix)
    return inverses


def apply(rows, inverse):
    rh, rm, rl = split3(rows)
    xh, xm, xl = split3(inverse)
    return dot(across([rh, rh, rh, rm, rm, rl]), down([xh, xm, xl, xh, xm, xh]))


def kernel(
    quads, tiles,
    offsets_hbm, leaf_hbm, node_hbm, pair_hbm, group_hbm, blocks_hbm, sketch_hbm,
    leaf_result, node_result, node_rows, pair_rows, group_rows,
    window, mats, offsets, leaf_index, node_index, pair_index, group_index, pivots, pick_leaf, pick_up, pick_send, partial,
    skel, coupling, node_coupling, start,
    local_sem, index_sem, send_sem, recv_sem, up_send, up_recv,
):
    q = lax.axis_index("quad")
    t = lax.axis_index("tile")
    me = q * tiles + t
    last = quads * tiles - 1
    odd = t % 2
    even = 1 - odd

    def at(flat):
        return (flat // tiles, flat % tiles)

    sibling = (q, t + 1 - 2 * odd)
    pair_of = t // 2
    other_pair = pair_of + 1 - 2 * (pair_of % 2)
    cousins = [(q, 2 * other_pair), (q, 2 * other_pair + 1)]
    partners = cousins + [sibling]

    barrier = pltpu.get_barrier_semaphore()

    @pl.when(me > 0)
    def _():
        pl.semaphore_signal(barrier, inc=1, device_id=at(me - 1), device_id_type=MESH)

    @pl.when(me < last)
    def _():
        pl.semaphore_signal(barrier, inc=1, device_id=at(me + 1), device_id_type=MESH)

    for partner in partners:
        pl.semaphore_signal(barrier, inc=1, device_id=partner, device_id_type=MESH)

    smalls = [
        pltpu.make_async_copy(offsets_hbm, offsets, index_sem.at[0]),
        pltpu.make_async_copy(leaf_hbm, leaf_index, index_sem.at[1]),
        pltpu.make_async_copy(node_hbm, node_index, index_sem.at[2]),
        pltpu.make_async_copy(pair_hbm, pair_index, index_sem.at[3]),
        pltpu.make_async_copy(group_hbm, group_index, index_sem.at[4]),
    ]
    for small in smalls:
        small.start()
    own = pltpu.make_async_copy(sketch_hbm, window.at[pl.ds(HALF, LEAVES)], local_sem.at[LEAVES])
    own.start()

    def leaf_at(s):
        return even * (LEAVES - 1 - s) + odd * s

    def load(i):
        return pltpu.make_async_copy(blocks_hbm.at[i], mats.at[i], local_sem.at[i])

    for s in range(LEAVES):
        load(leaf_at(s)).start()

    ends = jnp.where(me > 0, 1, 0) + jnp.where(me < last, 1, 0)
    pl.semaphore_wait(barrier, 3 + ends)

    def to_right(j):
        return pltpu.make_async_remote_copy(
            src_ref=sketch_hbm.at[LEAVES - 1 - j], dst_ref=window.at[HALF - 1 - j],
            send_sem=send_sem.at[j], recv_sem=recv_sem.at[HALF - 1 - j],
            device_id=at(me + 1), device_id_type=MESH,
        )

    def to_left(j):
        return pltpu.make_async_remote_copy(
            src_ref=sketch_hbm.at[j], dst_ref=window.at[HALF + LEAVES + j],
            send_sem=send_sem.at[HALF + j], recv_sem=recv_sem.at[HALF + j],
            device_id=at(me - 1), device_id_type=MESH,
        )

    @pl.when(me < last)
    def _():
        for j in range(HALF):
            to_right(j).start()

    @pl.when(me > 0)
    def _():
        for j in range(HALF):
            to_left(j).start()

    @pl.when(me == 0)
    def _():
        window[0:HALF] = jnp.zeros((HALF, BLOCK, COLS), BF16)

    @pl.when(me == last)
    def _():
        window[HALF + LEAVES:] = jnp.zeros((HALF, BLOCK, COLS), BF16)

    for small in smalls:
        small.wait()
    pivots[...] = jnp.full((8, 128), -1.0, F32)
    pivots[0:4, :] = leaf_index[...].astype(F32)
    pivots[4:5, :] = node_index[...].astype(F32)
    pivots[5:6, 0:64] = pair_index[...].astype(F32)
    pivots[6:7, 0:32] = group_index[...].astype(F32)

    def one_hot(row, width):
        down = jnp.broadcast_to(pivots[row:row + 1, :], (128, 128)).T
        down = jnp.concatenate([down] * (width // 128), axis=1)
        lane = lax.broadcasted_iota(jnp.int32, (128, width), 1).astype(F32)
        return jnp.where(down == lane, 1.0, 0.0).astype(BF16)

    for i in range(LEAVES):
        pick_leaf[i] = one_hot(i, BLOCK)
    node_pick = one_hot(4, LEAVES * SKEL)
    upper_pick = dot(one_hot(5, SKEL)[0:64], node_pick).astype(BF16)
    higher_pick = dot(one_hot(6, 128)[0:32, 0:64], upper_pick).astype(BF16)
    pick_up[...] = node_pick
    both_pick = jnp.concatenate([upper_pick, higher_pick], axis=0)
    for i in range(LEAVES):
        pick_send[i] = dot(both_pick[:, i * SKEL:(i + 1) * SKEL], pick_leaf[i]).astype(BF16)
    partial[...] = jnp.zeros_like(partial)

    own.wait()

    def arrived(slot, which):
        return pltpu.make_async_remote_copy(
            src_ref=window.at[slot], dst_ref=window.at[slot],
            send_sem=send_sem.at[0], recv_sem=recv_sem.at[which],
            device_id=sibling, device_id_type=MESH,
        )

    for j in range(HALF):
        arrived(j + (HALF + LEAVES) * even, j + HALF * even).wait_recv()

    def term(i, j):
        k = even * (NNZ - 1 - j) + odd * j
        near = offsets[i, k] == k - HALF
        panel = jnp.where(near, window[i + k], window[i + k + 1])
        return dot(mats[i, k], panel)

    def first_terms(i):
        load(i).wait()
        total = term(i, 0)
        for j in range(1, NNZ - 1):
            total = total + term(i, j)
        return total

    def last_term(s, i, total):
        if s > 0:
            @pl.when((me > 0) & (me < last))
            def _():
                arrived(even * (HALF - s) + odd * (HALF + LEAVES - 1 + s),
                        even * (HALF - s) + odd * (HALF - 1 + s)).wait_recv()
        high, low = split(total + term(i, NNZ - 1))
        partial[0] += dot(pick_send[i], high)
        partial[1] += dot(pick_send[i], low)
        return high, low

    def leaf_stage(s, i, high, low):
        pick = pick_leaf[i]
        skel_high = dot(pick, high).astype(BF16)
        skel_low = dot(pick, low).astype(BF16)
        skel[0, i] = skel_high
        skel[1, i] = skel_low
        matrix, scale = normalized(gram(skel_high, skel_low, skel_high, skel_low))
        start[s] = matrix
        coupling[s] = gram(high, low, skel_high, skel_low) * scale

    for s in range(LEAVES - 1):
        i = leaf_at(s)
        high, low = last_term(s, i, first_terms(i))
        leaf_stage(s, i, high, low)

    inverses = invert([start[s] for s in range(LEAVES - 1)])
    for s in range(LEAVES - 1):
        i = leaf_at(s)
        leaf_result[i] = apply(coupling[s], inverses[s])

    s = LEAVES - 1
    i = leaf_at(s)
    high, low = last_term(s, i, first_terms(i))
    place = t % 4
    for part in range(2):
        pair_rows[odd, part] = partial[part, 0:64].astype(BF16)
        group_rows[place, part] = partial[part, 64:96].astype(BF16)

    sends = []
    for n, partner in enumerate(partners):
        sends.append(
            pltpu.make_async_remote_copy(
                src_ref=group_rows.at[place], dst_ref=group_rows.at[place],
                send_sem=up_send.at[1 + n], recv_sem=up_recv.at[1 + place],
                device_id=partner, device_id_type=MESH,
            )
        )
    sends.append(
        pltpu.make_async_remote_copy(
            src_ref=pair_rows.at[odd], dst_ref=pair_rows.at[odd],
            send_sem=up_send.at[0], recv_sem=up_recv.at[0],
            device_id=sibling, device_id_type=MESH,
        )
    )
    for send in sends:
        send.start()
    leaf_stage(s, i, high, low)
    all_high = skel[0].reshape(LEAVES * SKEL, COLS)
    all_low = skel[1].reshape(LEAVES * SKEL, COLS)
    node_high = dot(pick_up[...], all_high).astype(BF16)
    node_low = dot(pick_up[...], all_low).astype(BF16)
    node_rows[0] = node_high
    node_rows[1] = node_low
    matrix, scale = normalized(gram(node_high, node_low, node_high, node_low))
    node_coupling[...] = gram(all_high, all_low, node_high, node_low) * scale
    inverses = invert([start[LEAVES - 1], matrix])
    leaf_result[i] = apply(coupling[s], inverses[0])
    node_result[...] = apply(node_coupling[...], inverses[1])

    pltpu.make_async_remote_copy(
        src_ref=pair_rows.at[even], dst_ref=pair_rows.at[even],
        send_sem=up_send.at[0], recv_sem=up_recv.at[0],
        device_id=sibling, device_id_type=MESH,
    ).wait_recv()
    for n in range(1, 4):
        spot = (place + n) % 4
        pltpu.make_async_remote_copy(
            src_ref=group_rows.at[spot], dst_ref=group_rows.at[spot],
            send_sem=up_send.at[0], recv_sem=up_recv.at[1 + spot],
            device_id=sibling, device_id_type=MESH,
        ).wait_recv()

    @pl.when(me < last)
    def _():
        for j in range(HALF):
            to_right(j).wait_send()

    @pl.when(me > 0)
    def _():
        for j in range(HALF):
            to_left(j).wait_send()

    for send in sends:
        send.wait_send()


def finish(
    node_rows, pair_rows, group_rows, leaf_result, node_result,
    leaf_hbm, node_hbm, pairs_hbm, groups_hbm, pairs_out, groups_out, out_sem,
):
    puts = [
        pltpu.make_async_copy(leaf_result, leaf_hbm, out_sem.at[0]),
        pltpu.make_async_copy(node_result, node_hbm, out_sem.at[1]),
        pltpu.make_async_copy(pairs_out, pairs_hbm, out_sem.at[2]),
        pltpu.make_async_copy(groups_out, groups_hbm, out_sem.at[3]),
    ]
    puts[0].start()
    puts[1].start()
    odd = lax.axis_index("tile") % 2
    group_high = jnp.concatenate([group_rows[g, 0] for g in range(4)], axis=0)
    group_low = jnp.concatenate([group_rows[g, 1] for g in range(4)], axis=0)
    pair_high = jnp.concatenate([pair_rows[0, 0], pair_rows[1, 0]], axis=0)
    pair_low = jnp.concatenate([pair_rows[0, 1], pair_rows[1, 1]], axis=0)
    group_matrix, scale = normalized(gram(group_high, group_low, group_high, group_low))
    group_coupling = gram(pair_rows[odd, 0], pair_rows[odd, 1], group_high, group_low) * scale
    pair_matrix, scale = normalized(gram(pair_high, pair_low, pair_high, pair_low))
    pair_coupling = gram(node_rows[0], node_rows[1], pair_high, pair_low) * scale
    inverses = invert([pair_matrix, group_matrix])
    pairs_out[...] = apply(pair_coupling, inverses[0])
    puts[2].start()
    groups_out[...] = apply(group_coupling, inverses[1])
    puts[3].start()
    for put in puts:
        put.wait()


def body(quads, tiles, blocks, offsets, sketch, leaf_pivots, node_pivots, pair_pivots, group_pivots):
    any_space = pl.BlockSpec(memory_space=pl.ANY)
    vmem = pl.BlockSpec(memory_space=pltpu.VMEM)
    hbm = pl.BlockSpec(memory_space=pltpu.HBM)
    dma = pltpu.SemaphoreType.DMA
    leaf_shape = ((LEAVES, BLOCK, SKEL), F32)
    node_shape = ((LEAVES * SKEL, SKEL), F32)
    rows_shape = ((2, SKEL, COLS), BF16)
    pair_shape = ((2, 2, SKEL // 2, COLS), BF16)
    group_shape = ((4, 2, SKEL // 4, COLS), BF16)
    shapes = [leaf_shape, node_shape, rows_shape, pair_shape, group_shape]
    leaf_result, node_result, node_rows, pair_rows, group_rows = pl.pallas_call(
        functools.partial(kernel, quads, tiles),
        out_shape=[jax.ShapeDtypeStruct(s, d) for s, d in shapes],
        in_specs=[hbm] * 7,
        out_specs=[vmem] * 5,
        scratch_shapes=[
            pltpu.VMEM((LEAVES + 2 * HALF, BLOCK, COLS), BF16),
            pltpu.VMEM((LEAVES, NNZ, BLOCK, BLOCK), BF16),
            pltpu.SMEM((LEAVES, NNZ), jnp.int32),
            pltpu.VMEM((LEAVES, 128), jnp.int32),
            pltpu.VMEM((1, 128), jnp.int32),
            pltpu.VMEM((1, 64), jnp.int32),
            pltpu.VMEM((1, 32), jnp.int32),
            pltpu.VMEM((8, 128), F32),
            pltpu.VMEM((LEAVES, SKEL, BLOCK), BF16),
            pltpu.VMEM((SKEL, LEAVES * SKEL), BF16),
            pltpu.VMEM((LEAVES, 96, BLOCK), BF16),
            pltpu.VMEM((2, 96, COLS), F32),
            pltpu.VMEM((2, LEAVES, SKEL, COLS), BF16),
            pltpu.VMEM((LEAVES, BLOCK, SKEL), F32),
            pltpu.VMEM((LEAVES * SKEL, SKEL), F32),
            pltpu.VMEM((LEAVES, SKEL, SKEL), F32),
            dma((LEAVES + 1,)), dma((5,)), dma((2 * HALF,)), dma((2 * HALF,)),
            dma((4,)), dma((5,)),
        ],
        compiler_params=pltpu.CompilerParams(collective_id=0, has_side_effects=True, vmem_limit_bytes=20 * 1024 * 1024),
        name="compress",
    )(*(pltpu.with_memory_space_constraint(x, pltpu.HBM) for x in (
        offsets, leaf_pivots, node_pivots, pair_pivots, group_pivots,
        blocks, sketch.reshape(LEAVES, BLOCK, COLS))))
    outs = [leaf_shape, node_shape, ((SKEL, SKEL), F32), ((SKEL // 2, SKEL), F32)]
    leaf, node, pairs, groups = pl.pallas_call(
        finish,
        out_shape=[jax.ShapeDtypeStruct(s, d) for s, d in outs],
        in_specs=[vmem] * 5,
        out_specs=[hbm] * 4,
        scratch_shapes=[
            pltpu.VMEM((SKEL, SKEL), F32),
            pltpu.VMEM((SKEL // 2, SKEL), F32),
            dma((4,)),
        ],
        compiler_params=pltpu.CompilerParams(vmem_limit_bytes=10 * 1024 * 1024),
        name="finish",
    )(node_rows, pair_rows, group_rows, leaf_result, node_result)
    return leaf.reshape(LEAVES * BLOCK, SKEL), node, pairs, groups


def solution(mesh):
    split_all = P(("quad", "tile"), None)
    placed = (P(("quad", "tile"), None, None, None),) + (split_all,) * 6
    run = functools.partial(body, mesh.shape["quad"], mesh.shape["tile"])
    return jax.shard_map(
        run, mesh=mesh, in_specs=placed, out_specs=(split_all,) * 4, check_vma=False
    )
```

```python
import functools

import jax
import jax.numpy as jnp
from jax import lax
from jax.experimental import pallas as pl
from jax.experimental.pallas import tpu as pltpu
from jax.sharding import PartitionSpec as P

HALF = 3
NNZ = 6
LEAVES = 4
BLOCK = 256
SKEL = 128
COLS = 512
STEPS = 6

F32 = jnp.float32
BF16 = jnp.bfloat16
MESH = pl.DeviceIdType.MESH
NN = (((1,), (0,)), ((), ()))
NT = (((1,), (1,)), ((), ()))


def dot(a, b, dims=NN):
    return lax.dot_general(a, b, dims, preferred_element_type=F32)


def split(x):
    high = x.astype(BF16)
    low = (x - high.astype(F32)).astype(BF16)
    return high, low


def eye():
    row = lax.broadcasted_iota(jnp.int32, (SKEL, SKEL), 0)
    col = lax.broadcasted_iota(jnp.int32, (SKEL, SKEL), 1)
    return row == col


def gram(rows_high, rows_low, skel_high, skel_low):
    count = rows_high.shape[0]
    left = jnp.concatenate([rows_high, rows_low], axis=0)
    right = jnp.concatenate([skel_high, skel_low], axis=0)
    full = dot(left, right, NT)
    return (full[:count, :SKEL] + full[count:, :SKEL]) + (
        full[:count, SKEL:] + full[count:, SKEL:]
    )


def normalized(moment):
    diagonal = eye()
    trace = jnp.sum(jnp.where(diagonal, moment, 0.0), keepdims=True)
    damping = trace / SKEL + 1e-06
    scale = 1.0 / (65.0 * damping)
    return (moment + jnp.where(diagonal, damping, 0.0)) * scale, scale


def split3(x):
    high = x.astype(BF16)
    rest = x - high.astype(F32)
    middle = rest.astype(BF16)
    low = (rest - middle.astype(F32)).astype(BF16)
    return high, middle, low


def across(parts):
    return jnp.concatenate(parts, axis=1)


def down(parts):
    return jnp.concatenate(parts, axis=0)


def pair_product(left_high, left_low, right_high, right_low):
    empty = jnp.zeros_like(right_low)
    both = dot(
        across([left_high, left_low]),
        down([across([right_high, right_low]), across([right_high, empty])]),
    )
    return both[:, :SKEL] + both[:, SKEL:]


def invert(matrices, fillers=()):
    unit = jnp.where(eye(), 1.0, 0.0)
    rho = 128.0 / 130.0
    ts = list(matrices)
    xs = [None] * len(ts)
    waiting = list(fillers)
    for step in range(STEPS):
        gain = 2.0 / (2.0 - rho * rho)
        rho = gain - 1.0
        products = []
        for t, x in zip(ts, xs):
            th, tl = split(t)
            if step == 0:
                products.append((pair_product(th, tl, th, tl), None))
                continue
            xh, xl = split(x)
            if step == STEPS - 1:
                products.append((None, pair_product(th, tl, xh, xl)))
                continue
            high = across([th, xh])
            both = dot(across([th, tl, th]), down([high, high, across([tl, xl])]))
            products.append((both[:, :SKEL], both[:, SKEL:]))
        if waiting:
            waiting.pop(0)()
        for j, (square, product) in enumerate(products):
            if step == 0:
                xs[j] = (2.0 * gain) * unit - gain * ts[j]
            else:
                xs[j] = (2.0 * gain) * xs[j] - gain * product
            if square is not None:
                ts[j] = (2.0 * gain) * ts[j] - gain * square
    pieces = []
    for x, matrix in zip(xs, matrices):
        xh, xl = split(x)
        high, middle, low = split3(matrix)
        parts = across([xh, xl])
        near = dot(across([high, middle]), down([parts, parts]))
        pieces.append((xh, xl, (near[:, :SKEL] + near[:, SKEL:]) + dot(low, xh)))
    for filler in waiting:
        filler()
    return [(xh, xl, unit - near) for xh, xl, near in pieces]


def corrected(near_inverse):
    xh, xl, rest = near_inverse
    eh, el = split(rest)
    return (xh.astype(F32) + xl.astype(F32)) + pair_product(xh, xl, eh, el)


def apply_near(rows, near_inverse):
    xh, xl, rest = near_inverse
    rh, rm, rl = split3(rows)
    parts = across([xh, xl])
    main = dot(across([rh, rm]), down([parts, parts]))
    product = (main[:, :SKEL] + main[:, SKEL:]) + dot(rl, xh)
    return product + pair_product(*split(product), *split(rest))


def apply(rows, inverse):
    rh, rm, rl = split3(rows)
    xh, xm, xl = split3(inverse)
    parts = across([xh, xm])
    main = dot(across([rh, rm]), down([parts, parts]))
    return (main[:, :SKEL] + main[:, SKEL:]) + dot(across([rh, rl]), down([xl, xh]))


def kernel(
    quads, tiles,
    offsets_hbm, leaf_hbm, node_hbm, pair_hbm, group_hbm, blocks_hbm, sketch_hbm,
    leaf_result, last_coupling, node_coupling, near, node_rows, pair_rows, group_rows,
    window, mats, offsets, leaf_index, node_index, pair_index, group_index, pivots, pick_leaf, pick_node, pick_send, partial, node_partial,
    skel, coupling, start,
    local_sem, index_sem, send_sem, recv_sem, up_send, up_recv,
):
    q = lax.axis_index("quad")
    t = lax.axis_index("tile")
    me = q * tiles + t
    last = quads * tiles - 1
    odd = t % 2
    even = 1 - odd

    def at(flat):
        return (flat // tiles, flat % tiles)

    sibling = (q, t + 1 - 2 * odd)
    pair_of = t // 2
    other_pair = pair_of + 1 - 2 * (pair_of % 2)
    cousins = [(q, 2 * other_pair), (q, 2 * other_pair + 1)]
    partners = cousins + [sibling]

    barrier = pltpu.get_barrier_semaphore()

    @pl.when(me > 0)
    def _():
        pl.semaphore_signal(barrier, inc=1, device_id=at(me - 1), device_id_type=MESH)

    @pl.when(me < last)
    def _():
        pl.semaphore_signal(barrier, inc=1, device_id=at(me + 1), device_id_type=MESH)

    for partner in partners:
        pl.semaphore_signal(barrier, inc=1, device_id=partner, device_id_type=MESH)

    smalls = [
        pltpu.make_async_copy(offsets_hbm, offsets, index_sem.at[0]),
        pltpu.make_async_copy(leaf_hbm, leaf_index, index_sem.at[1]),
        pltpu.make_async_copy(node_hbm, node_index, index_sem.at[2]),
        pltpu.make_async_copy(pair_hbm, pair_index, index_sem.at[3]),
        pltpu.make_async_copy(group_hbm, group_index, index_sem.at[4]),
    ]
    for small in smalls:
        small.start()
    def leaf_at(s):
        return even * (LEAVES - 1 - s) + odd * s

    def load(i):
        return pltpu.make_async_copy(blocks_hbm.at[i], mats.at[i], local_sem.at[i])

    ends = jnp.where(me > 0, 1, 0) + jnp.where(me < last, 1, 0)
    pl.semaphore_wait(barrier, 3 + ends)

    def to_right(j):
        return pltpu.make_async_remote_copy(
            src_ref=sketch_hbm.at[LEAVES - 1 - j], dst_ref=window.at[HALF - 1 - j],
            send_sem=send_sem.at[j], recv_sem=recv_sem.at[HALF - 1 - j],
            device_id=at(me + 1), device_id_type=MESH,
        )

    def to_left(j):
        return pltpu.make_async_remote_copy(
            src_ref=sketch_hbm.at[j], dst_ref=window.at[HALF + LEAVES + j],
            send_sem=send_sem.at[HALF + j], recv_sem=recv_sem.at[HALF + j],
            device_id=at(me - 1), device_id_type=MESH,
        )

    @pl.when(me < last)
    def _():
        for j in range(HALF):
            to_right(j).start()

    @pl.when(me > 0)
    def _():
        for j in range(HALF):
            to_left(j).start()

    own = pltpu.make_async_copy(sketch_hbm, window.at[pl.ds(HALF, LEAVES)], local_sem.at[LEAVES])
    own.start()

    for s in range(LEAVES):
        load(leaf_at(s)).start()

    @pl.when(me == 0)
    def _():
        window[0:HALF] = jnp.zeros((HALF, BLOCK, COLS), BF16)

    @pl.when(me == last)
    def _():
        window[HALF + LEAVES:] = jnp.zeros((HALF, BLOCK, COLS), BF16)

    for small in smalls:
        small.wait()
    pivots[...] = jnp.full((8, 128), -1.0, F32)
    pivots[0:4, :] = leaf_index[...].astype(F32)
    pivots[4:5, :] = node_index[...].astype(F32)
    pivots[5:6, 0:64] = pair_index[...].astype(F32)
    pivots[6:7, 0:32] = group_index[...].astype(F32)

    def one_hot(row, width):
        down = jnp.broadcast_to(pivots[row:row + 1, :], (128, 128)).T
        down = jnp.concatenate([down] * (width // 128), axis=1)
        lane = lax.broadcasted_iota(jnp.int32, (128, width), 1).astype(F32)
        return jnp.where(down == lane, 1.0, 0.0).astype(BF16)

    for i in range(LEAVES):
        pick_leaf[i] = one_hot(i, BLOCK)
    node_pick = one_hot(4, LEAVES * SKEL)
    upper_pick = dot(one_hot(5, SKEL)[0:64], node_pick).astype(BF16)
    higher_pick = dot(one_hot(6, 128)[0:32, 0:64], upper_pick).astype(BF16)
    both_pick = jnp.concatenate([upper_pick, higher_pick], axis=0)
    for i in range(LEAVES):
        pick_send[i] = dot(both_pick[:, i * SKEL:(i + 1) * SKEL], pick_leaf[i]).astype(BF16)
        pick_node[i] = dot(node_pick[:, i * SKEL:(i + 1) * SKEL], pick_leaf[i]).astype(BF16)
    partial[...] = jnp.zeros_like(partial)
    node_partial[...] = jnp.zeros_like(node_partial)

    own.wait()

    def arrived(slot, which):
        return pltpu.make_async_remote_copy(
            src_ref=window.at[slot], dst_ref=window.at[slot],
            send_sem=send_sem.at[0], recv_sem=recv_sem.at[which],
            device_id=sibling, device_id_type=MESH,
        )

    for j in range(HALF):
        arrived(j + (HALF + LEAVES) * even, j + HALF * even).wait_recv()

    def term(i, j):
        k = even * (NNZ - 1 - j) + odd * j
        near = offsets[i, k] == k - HALF
        panel = jnp.where(near, window[i + k], window[i + k + 1])
        return dot(mats[i, k], panel)

    def first_terms(i):
        load(i).wait()
        total = term(i, 0)
        for j in range(1, NNZ - 1):
            total = total + term(i, j)
        return total

    def last_term(s, i, total):
        if s > 0:
            @pl.when((me > 0) & (me < last))
            def _():
                arrived(even * (HALF - s) + odd * (HALF + LEAVES - 1 + s),
                        even * (HALF - s) + odd * (HALF - 1 + s)).wait_recv()
        high, low = split(total + term(i, NNZ - 1))
        partial[0] += dot(pick_send[i], high)
        partial[1] += dot(pick_send[i], low)
        return high, low

    def leaf_stage(s, i, high, low):
        pick = pick_leaf[i]
        skel_high = dot(pick, high).astype(BF16)
        skel_low = dot(pick, low).astype(BF16)
        skel[0, i] = skel_high
        skel[1, i] = skel_low
        matrix, scale = normalized(gram(skel_high, skel_low, skel_high, skel_low))
        start[s] = matrix

        def couple(first, count):
            part = gram(high[first:first + count], low[first:first + count], skel_high, skel_low)
            if s < LEAVES - 1:
                coupling[s, first:first + count] = part * scale
            else:
                last_coupling[first:first + count] = part * scale

        return [functools.partial(couple, first, 128) for first in (0, 128)]

    for s in range(LEAVES - 1):
        i = leaf_at(s)
        high, low = last_term(s, i, first_terms(i))
        node_partial[0] += dot(pick_node[i], high)
        node_partial[1] += dot(pick_node[i], low)
        for fill in leaf_stage(s, i, high, low):
            fill()

    inverses = invert([start[s] for s in range(LEAVES - 1)])
    for s in range(LEAVES - 1):
        i = leaf_at(s)
        leaf_result[i] = apply(coupling[s], corrected(inverses[s]))

    s = LEAVES - 1
    i = leaf_at(s)
    high, low = last_term(s, i, first_terms(i))
    place = t % 4
    for part in range(2):
        pair_rows[odd, part] = partial[part, 0:64].astype(BF16)
        group_rows[place, part] = partial[part, 64:96].astype(BF16)

    sends = []
    for n, partner in enumerate(partners):
        sends.append(
            pltpu.make_async_remote_copy(
                src_ref=group_rows.at[place], dst_ref=group_rows.at[place],
                send_sem=up_send.at[1 + n], recv_sem=up_recv.at[1 + place],
                device_id=partner, device_id_type=MESH,
            )
        )
    sends.append(
        pltpu.make_async_remote_copy(
            src_ref=pair_rows.at[odd], dst_ref=pair_rows.at[odd],
            send_sem=up_send.at[0], recv_sem=up_recv.at[0],
            device_id=sibling, device_id_type=MESH,
        )
    )
    for send in sends:
        send.start()
    fillers = leaf_stage(s, i, high, low)
    node_high = (node_partial[0] + dot(pick_node[i], high)).astype(BF16)
    node_low = (node_partial[1] + dot(pick_node[i], low)).astype(BF16)
    node_rows[0] = node_high
    node_rows[1] = node_low
    matrix, node_scale = normalized(gram(node_high, node_low, node_high, node_low))

    def couple_node(leaf):
        part = gram(skel[0, leaf], skel[1, leaf], node_high, node_low)
        node_coupling[leaf * SKEL:(leaf + 1) * SKEL] = part * node_scale

    fillers += [functools.partial(couple_node, leaf) for leaf in range(LEAVES)]
    inverses = invert([start[LEAVES - 1], matrix], fillers)
    for n, (xh, xl, rest) in enumerate(inverses):
        near[n, 0] = xh.astype(F32) + xl.astype(F32)
        near[n, 1] = rest

    pltpu.make_async_remote_copy(
        src_ref=pair_rows.at[even], dst_ref=pair_rows.at[even],
        send_sem=up_send.at[0], recv_sem=up_recv.at[0],
        device_id=sibling, device_id_type=MESH,
    ).wait_recv()
    for n in range(1, 4):
        spot = (place + n) % 4
        pltpu.make_async_remote_copy(
            src_ref=group_rows.at[spot], dst_ref=group_rows.at[spot],
            send_sem=up_send.at[0], recv_sem=up_recv.at[1 + spot],
            device_id=sibling, device_id_type=MESH,
        ).wait_recv()

    @pl.when(me < last)
    def _():
        for j in range(HALF):
            to_right(j).wait_send()

    @pl.when(me > 0)
    def _():
        for j in range(HALF):
            to_left(j).wait_send()

    for send in sends:
        send.wait_send()


def finish(
    leaf_result, last_coupling, node_coupling, near, node_rows, pair_rows, group_rows,
    leaf_hbm, node_hbm, pairs_hbm, groups_hbm, last_out, node_out, pairs_out, groups_out, out_sem,
):
    odd = lax.axis_index("tile") % 2
    first = 1 - odd
    last_leaf = odd * (LEAVES - 1)
    early = pltpu.make_async_copy(
        leaf_result.at[pl.ds(first, LEAVES - 1)], leaf_hbm.at[pl.ds(first, LEAVES - 1)], out_sem.at[0]
    )
    early.start()
    half = LEAVES * SKEL // 2
    puts = [pltpu.make_async_copy(last_out, leaf_hbm.at[last_leaf], out_sem.at[1])]
    for n in range(2):
        rows = pl.ds(half * n, half)
        puts.append(pltpu.make_async_copy(node_out.at[rows], node_hbm.at[rows], out_sem.at[2 + n]))
    puts.append(pltpu.make_async_copy(pairs_out, pairs_hbm, out_sem.at[4]))
    puts.append(pltpu.make_async_copy(groups_out, groups_hbm, out_sem.at[5]))
    group_high = jnp.concatenate([group_rows[g, 0] for g in range(4)], axis=0)
    group_low = jnp.concatenate([group_rows[g, 1] for g in range(4)], axis=0)
    pair_high = jnp.concatenate([pair_rows[0, 0], pair_rows[1, 0]], axis=0)
    pair_low = jnp.concatenate([pair_rows[0, 1], pair_rows[1, 1]], axis=0)
    group_matrix, group_scale = normalized(gram(group_high, group_low, group_high, group_low))
    pair_matrix, pair_scale = normalized(gram(pair_high, pair_low, pair_high, pair_low))
    coupled = []
    fixed = []

    def fix():
        for n in range(2):
            fixed.append(corrected((*split(near[n, 0]), near[n, 1])))

    def last_rows():
        last_out[...] = apply(last_coupling[...], fixed[0])
        puts[0].start()

    def node_part(n):
        rows = slice(half * n, half * n + half)
        node_out[rows] = apply(node_coupling[rows], fixed[1])
        puts[1 + n].start()

    inverses = invert([pair_matrix, group_matrix], [
        fix,
        functools.partial(node_part, 0),
        functools.partial(node_part, 1),
        last_rows,
        lambda: coupled.append(gram(node_rows[0], node_rows[1], pair_high, pair_low) * pair_scale),
        lambda: coupled.append(
            gram(pair_rows[odd, 0], pair_rows[odd, 1], group_high, group_low) * group_scale
        ),
    ])
    pair_coupling, group_coupling = coupled
    pairs_out[...] = apply_near(pair_coupling, inverses[0])
    puts[3].start()
    groups_out[...] = apply_near(group_coupling, inverses[1])
    puts[4].start()
    early.wait()
    for put in puts:
        put.wait()


def body(quads, tiles, blocks, offsets, sketch, leaf_pivots, node_pivots, pair_pivots, group_pivots):
    any_space = pl.BlockSpec(memory_space=pl.ANY)
    vmem = pl.BlockSpec(memory_space=pltpu.VMEM)
    hbm = pl.BlockSpec(memory_space=pltpu.HBM)
    dma = pltpu.SemaphoreType.DMA
    leaf_shape = ((LEAVES, BLOCK, SKEL), F32)
    node_shape = ((LEAVES * SKEL, SKEL), F32)
    rows_shape = ((2, SKEL, COLS), BF16)
    pair_shape = ((2, 2, SKEL // 2, COLS), BF16)
    group_shape = ((4, 2, SKEL // 4, COLS), BF16)
    block_shape = ((BLOCK, SKEL), F32)
    near_shape = ((2, 2, SKEL, SKEL), F32)
    shapes = [leaf_shape, block_shape, node_shape, near_shape, rows_shape, pair_shape, group_shape]
    results = pl.pallas_call(
        functools.partial(kernel, quads, tiles),
        out_shape=[jax.ShapeDtypeStruct(s, d) for s, d in shapes],
        in_specs=[hbm] * 7,
        out_specs=[vmem] * 7,
        scratch_shapes=[
            pltpu.VMEM((LEAVES + 2 * HALF, BLOCK, COLS), BF16),
            pltpu.VMEM((LEAVES, NNZ, BLOCK, BLOCK), BF16),
            pltpu.SMEM((LEAVES, NNZ), jnp.int32),
            pltpu.VMEM((LEAVES, 128), jnp.int32),
            pltpu.VMEM((1, 128), jnp.int32),
            pltpu.VMEM((1, 64), jnp.int32),
            pltpu.VMEM((1, 32), jnp.int32),
            pltpu.VMEM((8, 128), F32),
            pltpu.VMEM((LEAVES, SKEL, BLOCK), BF16),
            pltpu.VMEM((LEAVES, SKEL, BLOCK), BF16),
            pltpu.VMEM((LEAVES, 96, BLOCK), BF16),
            pltpu.VMEM((2, 96, COLS), F32),
            pltpu.VMEM((2, SKEL, COLS), F32),
            pltpu.VMEM((2, LEAVES, SKEL, COLS), BF16),
            pltpu.VMEM((LEAVES - 1, BLOCK, SKEL), F32),
            pltpu.VMEM((LEAVES, SKEL, SKEL), F32),
            dma((LEAVES + 1,)), dma((5,)), dma((2 * HALF,)), dma((2 * HALF,)),
            dma((4,)), dma((5,)),
        ],
        compiler_params=pltpu.CompilerParams(collective_id=0, has_side_effects=True, vmem_limit_bytes=20 * 1024 * 1024),
        name="compress",
    )(*(pltpu.with_memory_space_constraint(x, pltpu.HBM) for x in (
        offsets, leaf_pivots, node_pivots, pair_pivots, group_pivots,
        blocks, sketch.reshape(LEAVES, BLOCK, COLS))))
    outs = [leaf_shape, node_shape, ((SKEL, SKEL), F32), ((SKEL // 2, SKEL), F32)]
    leaf, node, pairs, groups = pl.pallas_call(
        finish,
        out_shape=[jax.ShapeDtypeStruct(s, d) for s, d in outs],
        in_specs=[vmem] * 7,
        out_specs=[hbm] * 4,
        scratch_shapes=[
            pltpu.VMEM(*block_shape),
            pltpu.VMEM(*node_shape),
            pltpu.VMEM((SKEL, SKEL), F32),
            pltpu.VMEM((SKEL // 2, SKEL), F32),
            dma((6,)),
        ],
        compiler_params=pltpu.CompilerParams(vmem_limit_bytes=10 * 1024 * 1024),
        name="finish",
    )(*results)
    return leaf.reshape(LEAVES * BLOCK, SKEL), node, pairs, groups


def solution(mesh):
    split_all = P(("quad", "tile"), None)
    placed = (P(("quad", "tile"), None, None, None),) + (split_all,) * 6
    run = functools.partial(body, mesh.shape["quad"], mesh.shape["tile"])
    return jax.shard_map(
        run, mesh=mesh, in_specs=placed, out_specs=(split_all,) * 4, check_vma=False
    )
```

```python
import functools

import jax
import jax.numpy as jnp
from jax import lax
from jax.experimental import pallas as pl
from jax.experimental.pallas import tpu as pltpu
from jax.sharding import PartitionSpec as P

HALF = 3
NNZ = 6
LEAVES = 4
BLOCK = 256
SKEL = 128
COLS = 512
STEPS = 6

F32 = jnp.float32
BF16 = jnp.bfloat16
MESH = pl.DeviceIdType.MESH
NN = (((1,), (0,)), ((), ()))
NT = (((1,), (1,)), ((), ()))


def dot(a, b, dims=NN):
    return lax.dot_general(a, b, dims, preferred_element_type=F32)


def split(x):
    high = x.astype(BF16)
    low = (x - high.astype(F32)).astype(BF16)
    return high, low


def eye():
    row = lax.broadcasted_iota(jnp.int32, (SKEL, SKEL), 0)
    col = lax.broadcasted_iota(jnp.int32, (SKEL, SKEL), 1)
    return row == col


def gram(rows_high, rows_low, skel_high, skel_low):
    count = rows_high.shape[0]
    left = jnp.concatenate([rows_high, rows_low], axis=0)
    right = jnp.concatenate([skel_high, skel_low], axis=0)
    full = dot(left, right, NT)
    return (full[:count, :SKEL] + full[count:, :SKEL]) + (
        full[:count, SKEL:] + full[count:, SKEL:]
    )


def normalized(moment):
    diagonal = eye()
    trace = jnp.sum(jnp.where(diagonal, moment, 0.0), keepdims=True)
    damping = trace / SKEL + 1e-06
    scale = 1.0 / (65.0 * damping)
    return (moment + jnp.where(diagonal, damping, 0.0)) * scale, scale


def split3(x):
    high = x.astype(BF16)
    rest = x - high.astype(F32)
    middle = rest.astype(BF16)
    low = (rest - middle.astype(F32)).astype(BF16)
    return high, middle, low


def across(parts):
    return jnp.concatenate(parts, axis=1)


def down(parts):
    return jnp.concatenate(parts, axis=0)


def pair_product(left_high, left_low, right_high, right_low):
    empty = jnp.zeros_like(right_low)
    both = dot(
        across([left_high, left_low]),
        down([across([right_high, right_low]), across([right_high, empty])]),
    )
    return both[:, :SKEL] + both[:, SKEL:]


def invert(matrices, fillers=()):
    unit = jnp.where(eye(), 1.0, 0.0)
    rho = 128.0 / 130.0
    ts = list(matrices)
    xs = [None] * len(ts)
    waiting = list(fillers)
    for step in range(STEPS):
        gain = 2.0 / (2.0 - rho * rho)
        rho = gain - 1.0
        products = []
        for t, x in zip(ts, xs):
            th, tl = split(t)
            if step == 0:
                products.append((pair_product(th, tl, th, tl), None))
                continue
            xh, xl = split(x)
            if step == STEPS - 1:
                products.append((None, pair_product(th, tl, xh, xl)))
                continue
            high = across([th, xh])
            both = dot(across([th, tl, th]), down([high, high, across([tl, xl])]))
            products.append((both[:, :SKEL], both[:, SKEL:]))
        if waiting:
            waiting.pop(0)()
        for j, (square, product) in enumerate(products):
            if step == 0:
                xs[j] = (2.0 * gain) * unit - gain * ts[j]
            else:
                xs[j] = (2.0 * gain) * xs[j] - gain * product
            if square is not None:
                ts[j] = (2.0 * gain) * ts[j] - gain * square
    pieces = []
    for x, matrix in zip(xs, matrices):
        xh, xl = split(x)
        high, middle, low = split3(matrix)
        parts = across([xh, xl])
        near = dot(across([high, middle]), down([parts, parts]))
        pieces.append((xh, xl, (near[:, :SKEL] + near[:, SKEL:]) + dot(low, xh)))
    for filler in waiting:
        filler()
    return [(xh, xl, unit - near) for xh, xl, near in pieces]


def corrected(near_inverse):
    xh, xl, rest = near_inverse
    eh, el = split(rest)
    return (xh.astype(F32) + xl.astype(F32)) + pair_product(xh, xl, eh, el)


def apply_near(rows, near_inverse):
    xh, xl, rest = near_inverse
    rh, rm, rl = split3(rows)
    parts = across([xh, xl])
    main = dot(across([rh, rm]), down([parts, parts]))
    product = (main[:, :SKEL] + main[:, SKEL:]) + dot(rl, xh)
    return product + pair_product(*split(product), *split(rest))


def apply(rows, inverse):
    rh, rm, rl = split3(rows)
    xh, xm, xl = split3(inverse)
    parts = across([xh, xm])
    main = dot(across([rh, rm]), down([parts, parts]))
    return (main[:, :SKEL] + main[:, SKEL:]) + dot(across([rh, rl]), down([xl, xh]))


def kernel(
    quads, tiles,
    offsets_hbm, leaf_hbm, node_hbm, pair_hbm, group_hbm, blocks_hbm, sketch_hbm,
    leaf_result, last_coupling, node_coupling, near, node_rows, pair_rows, group_rows,
    window, mats, offsets, leaf_index, node_index, pair_index, group_index, pivots, pick_leaf, pick_node, pick_send, partial, node_partial,
    skel, coupling, start,
    local_sem, index_sem, send_sem, recv_sem, up_send, up_recv,
):
    q = lax.axis_index("quad")
    t = lax.axis_index("tile")
    me = q * tiles + t
    last = quads * tiles - 1
    odd = t % 2
    even = 1 - odd

    def at(flat):
        return (flat // tiles, flat % tiles)

    sibling = (q, t + 1 - 2 * odd)
    pair_of = t // 2
    other_pair = pair_of + 1 - 2 * (pair_of % 2)
    cousins = [(q, 2 * other_pair), (q, 2 * other_pair + 1)]
    partners = cousins + [sibling]

    barrier = pltpu.get_barrier_semaphore()

    @pl.when(me > 0)
    def _():
        pl.semaphore_signal(barrier, inc=1, device_id=at(me - 1), device_id_type=MESH)

    @pl.when(me < last)
    def _():
        pl.semaphore_signal(barrier, inc=1, device_id=at(me + 1), device_id_type=MESH)

    for partner in partners:
        pl.semaphore_signal(barrier, inc=1, device_id=partner, device_id_type=MESH)

    smalls = [
        pltpu.make_async_copy(offsets_hbm, offsets, index_sem.at[0]),
        pltpu.make_async_copy(leaf_hbm, leaf_index, index_sem.at[1]),
        pltpu.make_async_copy(node_hbm, node_index, index_sem.at[2]),
        pltpu.make_async_copy(pair_hbm, pair_index, index_sem.at[3]),
        pltpu.make_async_copy(group_hbm, group_index, index_sem.at[4]),
    ]
    for small in smalls:
        small.start()
    def leaf_at(s):
        return even * (LEAVES - 1 - s) + odd * s

    def load(i):
        return pltpu.make_async_copy(blocks_hbm.at[i], mats.at[i], local_sem.at[i])

    ends = jnp.where(me > 0, 1, 0) + jnp.where(me < last, 1, 0)
    pl.semaphore_wait(barrier, 3 + ends)

    def to_right(j):
        return pltpu.make_async_remote_copy(
            src_ref=sketch_hbm.at[LEAVES - 1 - j], dst_ref=window.at[HALF - 1 - j],
            send_sem=send_sem.at[j], recv_sem=recv_sem.at[HALF - 1 - j],
            device_id=at(me + 1), device_id_type=MESH,
        )

    def to_left(j):
        return pltpu.make_async_remote_copy(
            src_ref=sketch_hbm.at[j], dst_ref=window.at[HALF + LEAVES + j],
            send_sem=send_sem.at[HALF + j], recv_sem=recv_sem.at[HALF + j],
            device_id=at(me - 1), device_id_type=MESH,
        )

    @pl.when(me < last)
    def _():
        for j in range(HALF):
            to_right(j).start()

    @pl.when(me > 0)
    def _():
        for j in range(HALF):
            to_left(j).start()

    own = pltpu.make_async_copy(sketch_hbm, window.at[pl.ds(HALF, LEAVES)], local_sem.at[LEAVES])
    own.start()

    for s in range(LEAVES):
        load(leaf_at(s)).start()

    @pl.when(me == 0)
    def _():
        window[0:HALF] = jnp.zeros((HALF, BLOCK, COLS), BF16)

    @pl.when(me == last)
    def _():
        window[HALF + LEAVES:] = jnp.zeros((HALF, BLOCK, COLS), BF16)

    for small in smalls:
        small.wait()
    pivots[...] = jnp.full((8, 128), -1.0, F32)
    pivots[0:4, :] = leaf_index[...].astype(F32)
    pivots[4:5, :] = node_index[...].astype(F32)
    pivots[5:6, 0:64] = pair_index[...].astype(F32)
    pivots[6:7, 0:32] = group_index[...].astype(F32)

    def one_hot(row, width):
        down = jnp.broadcast_to(pivots[row:row + 1, :], (128, 128)).T
        down = jnp.concatenate([down] * (width // 128), axis=1)
        lane = lax.broadcasted_iota(jnp.int32, (128, width), 1).astype(F32)
        return jnp.where(down == lane, 1.0, 0.0).astype(BF16)

    for i in range(LEAVES):
        pick_leaf[i] = one_hot(i, BLOCK)
    node_pick = one_hot(4, LEAVES * SKEL)
    upper_pick = dot(one_hot(5, SKEL)[0:64], node_pick).astype(BF16)
    higher_pick = dot(one_hot(6, 128)[0:32, 0:64], upper_pick).astype(BF16)
    both_pick = jnp.concatenate([upper_pick, higher_pick], axis=0)
    for i in range(LEAVES):
        pick_send[i] = dot(both_pick[:, i * SKEL:(i + 1) * SKEL], pick_leaf[i]).astype(BF16)
        pick_node[i] = dot(node_pick[:, i * SKEL:(i + 1) * SKEL], pick_leaf[i]).astype(BF16)
    partial[...] = jnp.zeros_like(partial)
    node_partial[...] = jnp.zeros_like(node_partial)

    own.wait()

    def arrived(slot, which):
        return pltpu.make_async_remote_copy(
            src_ref=window.at[slot], dst_ref=window.at[slot],
            send_sem=send_sem.at[0], recv_sem=recv_sem.at[which],
            device_id=sibling, device_id_type=MESH,
        )

    for j in range(HALF):
        arrived(j + (HALF + LEAVES) * even, j + HALF * even).wait_recv()

    def term(i, j):
        k = even * (NNZ - 1 - j) + odd * j
        near = offsets[i, k] == k - HALF
        panel = jnp.where(near, window[i + k], window[i + k + 1])
        return dot(mats[i, k], panel)

    def first_terms(i):
        load(i).wait()
        total = term(i, 0)
        for j in range(1, NNZ - 1):
            total = total + term(i, j)
        return total

    def panel_arrives(s):
        if s > 0:
            @pl.when((me > 0) & (me < last))
            def _():
                arrived(even * (HALF - s) + odd * (HALF + LEAVES - 1 + s),
                        even * (HALF - s) + odd * (HALF - 1 + s)).wait_recv()

    def leaf_stage(s, i, high, low):
        pick = pick_leaf[i]
        skel_high = dot(pick, high).astype(BF16)
        skel_low = dot(pick, low).astype(BF16)
        skel[0, i] = skel_high
        skel[1, i] = skel_low
        matrix, scale = normalized(gram(skel_high, skel_low, skel_high, skel_low))
        start[s] = matrix

        def couple(first, count):
            part = gram(high[first:first + count], low[first:first + count], skel_high, skel_low)
            if s < LEAVES - 1:
                coupling[s, first:first + count] = part * scale
            else:
                last_coupling[first:first + count] = part * scale

        return [functools.partial(couple, first, 128) for first in (0, 128)]

    for s in range(LEAVES - 1):
        i = leaf_at(s)
        total = first_terms(i)
        panel_arrives(s)
        high, low = split(total + term(i, NNZ - 1))
        partial[...] += dot(pick_send[i], high) + dot(pick_send[i], low)
        node_partial[0] += dot(pick_node[i], high)
        node_partial[1] += dot(pick_node[i], low)
        for fill in leaf_stage(s, i, high, low):
            fill()

    inverses = invert([start[s] for s in range(LEAVES - 1)])
    for s in range(LEAVES - 1):
        i = leaf_at(s)
        leaf_result[i] = apply(coupling[s], corrected(inverses[s]))

    s = LEAVES - 1
    i = leaf_at(s)
    total = first_terms(i)
    block = odd * (NNZ - 1)
    picked = dot(pick_send[i], mats[i, block]).astype(BF16)
    high, low = split(total)
    rows = partial[...] + (dot(pick_send[i], high) + dot(pick_send[i], low))
    partial[...] = rows
    panel_arrives(s)
    near_panel = offsets[i, block] == block - HALF
    panel = jnp.where(near_panel, window[i + block], window[i + block + 1])
    place = t % 4
    for part, value in enumerate(split(partial[...] + dot(picked, panel))):
        pair_rows[odd, part] = value[0:64]
        group_rows[place, part] = value[64:96]

    sends = []
    for n, partner in enumerate(partners):
        sends.append(
            pltpu.make_async_remote_copy(
                src_ref=group_rows.at[place], dst_ref=group_rows.at[place],
                send_sem=up_send.at[1 + n], recv_sem=up_recv.at[1 + place],
                device_id=partner, device_id_type=MESH,
            )
        )
    sends.append(
        pltpu.make_async_remote_copy(
            src_ref=pair_rows.at[odd], dst_ref=pair_rows.at[odd],
            send_sem=up_send.at[0], recv_sem=up_recv.at[0],
            device_id=sibling, device_id_type=MESH,
        )
    )
    for send in sends:
        send.start()
    high, low = split(total + dot(mats[i, block], panel))
    fillers = leaf_stage(s, i, high, low)
    node_high = (node_partial[0] + dot(pick_node[i], high)).astype(BF16)
    node_low = (node_partial[1] + dot(pick_node[i], low)).astype(BF16)
    node_rows[0] = node_high
    node_rows[1] = node_low
    matrix, node_scale = normalized(gram(node_high, node_low, node_high, node_low))

    def couple_node(leaf):
        part = gram(skel[0, leaf], skel[1, leaf], node_high, node_low)
        node_coupling[leaf * SKEL:(leaf + 1) * SKEL] = part * node_scale

    fillers += [functools.partial(couple_node, leaf) for leaf in range(LEAVES)]
    inverses = invert([start[LEAVES - 1], matrix], fillers)
    for n, (xh, xl, rest) in enumerate(inverses):
        near[n, 0] = xh.astype(F32) + xl.astype(F32)
        near[n, 1] = rest

    pltpu.make_async_remote_copy(
        src_ref=pair_rows.at[even], dst_ref=pair_rows.at[even],
        send_sem=up_send.at[0], recv_sem=up_recv.at[0],
        device_id=sibling, device_id_type=MESH,
    ).wait_recv()
    for n in range(1, 4):
        spot = (place + n) % 4
        pltpu.make_async_remote_copy(
            src_ref=group_rows.at[spot], dst_ref=group_rows.at[spot],
            send_sem=up_send.at[0], recv_sem=up_recv.at[1 + spot],
            device_id=sibling, device_id_type=MESH,
        ).wait_recv()

    @pl.when(me < last)
    def _():
        for j in range(HALF):
            to_right(j).wait_send()

    @pl.when(me > 0)
    def _():
        for j in range(HALF):
            to_left(j).wait_send()

    for send in sends:
        send.wait_send()


def finish(
    leaf_result, last_coupling, node_coupling, near, node_rows, pair_rows, group_rows,
    leaf_hbm, node_hbm, pairs_hbm, groups_hbm, last_out, node_out, pairs_out, groups_out, out_sem,
):
    odd = lax.axis_index("tile") % 2
    first = 1 - odd
    last_leaf = odd * (LEAVES - 1)
    early = pltpu.make_async_copy(
        leaf_result.at[pl.ds(first, LEAVES - 1)], leaf_hbm.at[pl.ds(first, LEAVES - 1)], out_sem.at[0]
    )
    early.start()
    half = LEAVES * SKEL // 2
    puts = [pltpu.make_async_copy(last_out, leaf_hbm.at[last_leaf], out_sem.at[1])]
    for n in range(2):
        rows = pl.ds(half * n, half)
        puts.append(pltpu.make_async_copy(node_out.at[rows], node_hbm.at[rows], out_sem.at[2 + n]))
    puts.append(pltpu.make_async_copy(pairs_out, pairs_hbm, out_sem.at[4]))
    puts.append(pltpu.make_async_copy(groups_out, groups_hbm, out_sem.at[5]))
    group_high = jnp.concatenate([group_rows[g, 0] for g in range(4)], axis=0)
    group_low = jnp.concatenate([group_rows[g, 1] for g in range(4)], axis=0)
    pair_high = jnp.concatenate([pair_rows[0, 0], pair_rows[1, 0]], axis=0)
    pair_low = jnp.concatenate([pair_rows[0, 1], pair_rows[1, 1]], axis=0)
    group_matrix, group_scale = normalized(gram(group_high, group_low, group_high, group_low))
    pair_matrix, pair_scale = normalized(gram(pair_high, pair_low, pair_high, pair_low))
    coupled = []
    fixed = []

    def fix():
        for n in range(2):
            fixed.append(corrected((*split(near[n, 0]), near[n, 1])))

    def last_rows():
        last_out[...] = apply(last_coupling[...], fixed[0])
        puts[0].start()

    def node_part(n):
        rows = slice(half * n, half * n + half)
        node_out[rows] = apply(node_coupling[rows], fixed[1])
        puts[1 + n].start()

    inverses = invert([pair_matrix, group_matrix], [
        fix,
        functools.partial(node_part, 0),
        functools.partial(node_part, 1),
        last_rows,
        lambda: coupled.append(gram(node_rows[0], node_rows[1], pair_high, pair_low) * pair_scale),
        lambda: coupled.append(
            gram(pair_rows[odd, 0], pair_rows[odd, 1], group_high, group_low) * group_scale
        ),
    ])
    pair_coupling, group_coupling = coupled
    pairs_out[...] = apply_near(pair_coupling, inverses[0])
    puts[3].start()
    groups_out[...] = apply_near(group_coupling, inverses[1])
    puts[4].start()
    early.wait()
    for put in puts:
        put.wait()


def body(quads, tiles, blocks, offsets, sketch, leaf_pivots, node_pivots, pair_pivots, group_pivots):
    any_space = pl.BlockSpec(memory_space=pl.ANY)
    vmem = pl.BlockSpec(memory_space=pltpu.VMEM)
    hbm = pl.BlockSpec(memory_space=pltpu.HBM)
    dma = pltpu.SemaphoreType.DMA
    leaf_shape = ((LEAVES, BLOCK, SKEL), F32)
    node_shape = ((LEAVES * SKEL, SKEL), F32)
    rows_shape = ((2, SKEL, COLS), BF16)
    pair_shape = ((2, 2, SKEL // 2, COLS), BF16)
    group_shape = ((4, 2, SKEL // 4, COLS), BF16)
    block_shape = ((BLOCK, SKEL), F32)
    near_shape = ((2, 2, SKEL, SKEL), F32)
    shapes = [leaf_shape, block_shape, node_shape, near_shape, rows_shape, pair_shape, group_shape]
    results = pl.pallas_call(
        functools.partial(kernel, quads, tiles),
        out_shape=[jax.ShapeDtypeStruct(s, d) for s, d in shapes],
        in_specs=[hbm] * 7,
        out_specs=[vmem] * 7,
        scratch_shapes=[
            pltpu.VMEM((LEAVES + 2 * HALF, BLOCK, COLS), BF16),
            pltpu.VMEM((LEAVES, NNZ, BLOCK, BLOCK), BF16),
            pltpu.SMEM((LEAVES, NNZ), jnp.int32),
            pltpu.VMEM((LEAVES, 128), jnp.int32),
            pltpu.VMEM((1, 128), jnp.int32),
            pltpu.VMEM((1, 64), jnp.int32),
            pltpu.VMEM((1, 32), jnp.int32),
            pltpu.VMEM((8, 128), F32),
            pltpu.VMEM((LEAVES, SKEL, BLOCK), BF16),
            pltpu.VMEM((LEAVES, SKEL, BLOCK), BF16),
            pltpu.VMEM((LEAVES, 96, BLOCK), BF16),
            pltpu.VMEM((96, COLS), F32),
            pltpu.VMEM((2, SKEL, COLS), F32),
            pltpu.VMEM((2, LEAVES, SKEL, COLS), BF16),
            pltpu.VMEM((LEAVES - 1, BLOCK, SKEL), F32),
            pltpu.VMEM((LEAVES, SKEL, SKEL), F32),
            dma((LEAVES + 1,)), dma((5,)), dma((2 * HALF,)), dma((2 * HALF,)),
            dma((4,)), dma((5,)),
        ],
        compiler_params=pltpu.CompilerParams(collective_id=0, has_side_effects=True, vmem_limit_bytes=20 * 1024 * 1024),
        name="compress",
    )(*(pltpu.with_memory_space_constraint(x, pltpu.HBM) for x in (
        offsets, leaf_pivots, node_pivots, pair_pivots, group_pivots,
        blocks, sketch.reshape(LEAVES, BLOCK, COLS))))
    outs = [leaf_shape, node_shape, ((SKEL, SKEL), F32), ((SKEL // 2, SKEL), F32)]
    leaf, node, pairs, groups = pl.pallas_call(
        finish,
        out_shape=[jax.ShapeDtypeStruct(s, d) for s, d in outs],
        in_specs=[vmem] * 7,
        out_specs=[hbm] * 4,
        scratch_shapes=[
            pltpu.VMEM(*block_shape),
            pltpu.VMEM(*node_shape),
            pltpu.VMEM((SKEL, SKEL), F32),
            pltpu.VMEM((SKEL // 2, SKEL), F32),
            dma((6,)),
        ],
        compiler_params=pltpu.CompilerParams(vmem_limit_bytes=10 * 1024 * 1024),
        name="finish",
    )(*results)
    return leaf.reshape(LEAVES * BLOCK, SKEL), node, pairs, groups


def solution(mesh):
    split_all = P(("quad", "tile"), None)
    placed = (P(("quad", "tile"), None, None, None),) + (split_all,) * 6
    run = functools.partial(body, mesh.shape["quad"], mesh.shape["tile"])
    return jax.shard_map(
        run, mesh=mesh, in_specs=placed, out_specs=(split_all,) * 4, check_vma=False
    )
```
